32 devices in a mesh: grp: 2 (over y), date: 4 (over z), row: 4 (over x, core).
Axes of the slice: x: 2, y: 2, z: 4, core: 2. Of those that a mesh axis runs over, the one named last changes fastest.
Arguments:
- stack_data: float32 [16, 2, 64, 512], P(('grp', 'date'), None, 'row'), parts along dimension 0, may hold values from -40 to 40, as said below
- plan: int32 [8], replicated, may hold values from 0 to 7, each once
Outputs:
- coherence: float32 [16, 8, 2, 64, 512], P(('grp', 'date'), None, None, 'row'), parts along dimension 0
The draws below stay inside these ranges and needn't reach their ends.
There are 2 independent parts, one for each index of `grp`. The reference program is written for one: setup_inputs(seed, part) draws one part's arguments, and reference() takes and returns one part's arrays. A program takes and returns all parts, laid end to end along the dimension named above; an argument that names none is the same for every part. Nothing has to cross between parts.
Inputs may be any that keep to these rules, and one draw needn't show every extreme that they name: `stack_data`: complex samples of one scene seen on every date, each date with its own phase, strength and noise.
All inputs are finite; a program needn't handle non-finite values.
Results may differ from the reference program's by a relative error of at most 0.00005.
Values sent between devices are 32-bit elements; how exact they have to be, the bound alone decides.
A program may use at most 64 MiB of HBM per device.

```python
import jax
import jax.numpy as jnp
from jax import lax

COLS = 512
HALF_ROWS = 4
HALF_COLS = 16
DATES = 8
ROWS = 64


def draw_stack_data(key, part):
    keys = jax.random.split(jax.random.fold_in(key, 17), 5)
    scene = jax.random.normal(keys[0], (2, ROWS, COLS), jnp.float32)
    phase = jax.random.uniform(keys[1], (DATES, 1, 1), jnp.float32, -3.14159, 3.14159)
    strength = jax.random.uniform(keys[2], (DATES, 1, 1), jnp.float32, 0.3, 1.5)
    noise_level = jnp.exp(jax.random.uniform(keys[3], (DATES, 1, 1, 1), jnp.float32, jnp.log(0.3), jnp.log(2.0)))
    noise = jax.random.normal(keys[4], (DATES, 2, ROWS, COLS), jnp.float32)
    turned_real = jnp.cos(phase) * scene[0][None] - jnp.sin(phase) * scene[1][None]
    turned_imag = jnp.sin(phase) * scene[0][None] + jnp.cos(phase) * scene[1][None]
    signal = strength[:, None] * jnp.stack([turned_real, turned_imag], axis=1)
    values = signal + noise_level * noise
    return jnp.clip(values, -40.0, 40.0)


def setup_inputs(seed: int = 0, part: int = 0) -> dict:
    arg_keys = jax.random.split(jax.random.key(seed), 3)
    part_keys = jax.random.split(jax.random.fold_in(arg_keys[2], part), 3)
    stack_data = draw_stack_data(jax.random.fold_in(jax.random.fold_in(arg_keys[2], part), 71), part)
    plan = jax.random.permutation(arg_keys[1], DATES).astype(jnp.int32)
    return {"stack_data": stack_data, "plan": plan}


def window_sum(field):
    lead = [(0, 0)] * (field.ndim - 2)
    padded = jnp.pad(field, lead + [(HALF_ROWS + 1, HALF_ROWS), (HALF_COLS + 1, HALF_COLS)])
    rowsum = jnp.cumsum(padded, axis=-2)
    rowsum = rowsum[..., 2 * HALF_ROWS + 1:, :] - rowsum[..., :ROWS, :]
    colsum = jnp.cumsum(rowsum, axis=-1)
    return colsum[..., 2 * HALF_COLS + 1:] - colsum[..., :COLS]

def reference(stack_data, plan):
    real_part = stack_data[:, 0]
    imag_part = stack_data[:, 1]
    power = window_sum(real_part * real_part + imag_part * imag_part)
    order_real = real_part[plan]
    order_imag = imag_part[plan]
    order_power = power[plan]

    def one_date(which):
        base_real = real_part[which]
        base_imag = imag_part[which]
        cross_real = window_sum(base_real[None] * order_real + base_imag[None] * order_imag)
        cross_imag = window_sum(base_imag[None] * order_real - base_real[None] * order_imag)
        factor = 1.0 / jnp.sqrt(power[which][None] * order_power + 1e-06)
        return jnp.stack([cross_real * factor, cross_imag * factor], axis=1)
    return lax.map(one_date, jnp.arange(DATES, dtype=jnp.int32))
```

```python
import functools

import jax
import jax.numpy as jnp
from jax import lax
from jax.experimental import pallas as pl
from jax.experimental.pallas import tpu as pltpu
from jax.sharding import PartitionSpec as P

HALF_ROWS = 4
HALF_COLS = 16
LANES = 128

epsilon = 1e-06


EDGE, MID = 0, 1


def chain_of_four():
    def send(s, k, d):
        return ("send", s, k, d)

    def take(s, k):
        return ("take", s, k)

    own_right = {d: [send(d, EDGE, d + 1), send(d, MID, d + 1)] for d in range(3)}
    enter = [("load",), ("down",), ("right",)]
    spots = {}
    for core in range(2):
        spots[0, core] = [enter, own_right[0]]
        spots[3, core] = [[("load",), ("down",)], []]
    spots[0, 0] += [[take(1, EDGE), take(2, EDGE)], [take(3, EDGE)], []]
    spots[0, 1] += [[take(1, EDGE)], [take(2, EDGE), take(3, EDGE)], []]
    for core in range(2):
        spots[3, core] += [[take(2, EDGE), take(1, EDGE)], [take(0, EDGE)], []]
    spots[3, 0][0] = [send(3, EDGE, 0), send(3, EDGE, 2), send(3, MID, 0), send(3, MID, 2), send(3, EDGE, 1),
                      send(3, MID, 1)] + spots[3, 0][0]
    spots[3, 1][0] = [send(3, EDGE, 2), send(3, MID, 2)] + spots[3, 1][0]
    first = [send(1, EDGE, 0), send(1, MID, 0)] + enter + own_right[1]
    spots[1, 0] = [first, [send(0, EDGE, 2), send(0, MID, 2)], [], [take(2, EDGE), take(3, EDGE)], []]
    spots[1, 1] = [first, [send(2, EDGE, 0), send(0, EDGE, 2), send(3, EDGE, 0), send(0, MID, 2), send(2, MID, 0),
                           send(3, MID, 0)], [], [], []]
    onward = [send(1, EDGE, 3), send(0, EDGE, 3), send(1, MID, 3), send(0, MID, 3)]
    spots[2, 0] = [[send(2, EDGE, 0), send(2, EDGE, 1), send(2, MID, 0)] + enter + own_right[2],
                   onward + [take(3, EDGE), send(2, MID, 1)], [], [], []]
    spots[2, 1] = [[send(2, EDGE, 1), send(2, MID, 1)] + enter + own_right[2],
                   [send(3, EDGE, 1), onward[0], send(3, MID, 1)] + onward[1:], [], [], []]
    return spots, {0: (1, 2, 3), 1: (0, 2, 3), 2: (1, 0, 3), 3: (2, 1, 0)}


def gather_kernel(n, rows_n, x_ref, coh, buf, top, bot, mine, other, band, pbuf, sbuf, lhs, pw,
                  load_sem, ready, recv, sent, rim_recv, rim_sent):
    local, _, height, width = x_ref.shape
    tiles = width // LANES
    span = height + 2 * HALF_ROWS
    me = lax.axis_index("date")
    row = lax.axis_index("row")
    has_left, has_right = me > 0, me < n - 1
    has_up, has_down = row > 0, row < rows_n - 1

    def count(*flags):
        return functools.reduce(jnp.add, [jnp.where(flag, 1, 0) for flag in flags])

    def tell(sem, axis, index):
        pl.semaphore_signal(sem, inc=1, device_id={axis: index}, device_id_type=pl.DeviceIdType.MESH)

    barrier = pltpu.get_barrier_semaphore()
    pl.when(has_down)(lambda: tell(barrier, "row", row + 1))
    load = pltpu.make_async_copy(x_ref, buf.at[pl.ds(me * local, local)], load_sem)
    load.start()
    pl.when(jnp.logical_or(has_left, has_up))(lambda: pl.semaphore_wait(barrier, count(has_left, has_up)))
    pl.when(has_right)(lambda: tell(barrier, "date", me + 1))
    pl.when(has_left)(lambda: tell(ready.at[0], "date", me - 1))
    pl.when(has_up)(lambda: tell(ready.at[1], "row", row - 1))

    def remote(src, dst, send_sem, recv_sem, axis, index):
        return pltpu.make_async_remote_copy(
            src_ref=src, dst_ref=dst, send_sem=send_sem, recv_sem=recv_sem,
            device_id={axis: index}, device_id_type=pl.DeviceIdType.MESH)

    upper, lower = slice(0, HALF_ROWS), slice(height - HALF_ROWS, height)
    middle = slice(HALF_ROWS, height - HALF_ROWS)

    def send(source, s, k, l, d, side):
        for rows in ((upper, lower), (middle,))[k]:
            remote(source.at[l, :, rows], buf.at[s * local + l, :, rows], sent.at[side], recv.at[s, k, l],
                   "date", d).start()

    def arrived(s, k, l):
        ref = buf.at[s * local + l, :, middle if k else slice(0, 2 * HALF_ROWS)]
        remote(ref, ref, sent.at[0], recv.at[s, k, l], "date", me).wait_recv()

    def all_sent(side, dates):
        ref = buf.at[pl.ds(0, dates)]
        remote(ref, ref, sent.at[side], sent.at[side], "date", me).wait_send()

    def rim_down(s, l):
        return remote(buf.at[s * local + l, :, lower], top.at[s, l], rim_sent.at[0], rim_recv.at[0, s, l], "row", row + 1)

    def rim_up(s, l):
        return remote(buf.at[s * local + l, :, upper], bot.at[s, l], rim_sent.at[1], rim_recv.at[1, s, l], "row", row - 1)

    def send_rims(s, l):
        pl.when(has_down)(lambda: rim_down(s, l).start())
        pl.when(has_up)(lambda: rim_up(s, l).start())

    def wait_rims(s, l):
        pl.when(has_up)(lambda: rim_down(s, l).wait_recv())
        pl.when(has_down)(lambda: rim_up(s, l).wait_recv())

    def prepare():
        @pl.when(row == 0)
        def _():
            top[...] = jnp.zeros_like(top)

        @pl.when(row == rows_n - 1)
        def _():
            bot[...] = jnp.zeros_like(bot)

        col_in = lax.broadcasted_iota(jnp.int32, (width, width), 0)
        col_out = lax.broadcasted_iota(jnp.int32, (width, width), 1)
        band[...] = jnp.where(jnp.abs(col_in - col_out) <= HALF_COLS, 1.0, 0.0).astype(jnp.bfloat16)

    def assemble(dst, s, l):
        low = height + HALF_ROWS
        for part in range(2):
            for c in range(tiles):
                lanes = slice(c * LANES, (c + 1) * LANES)
                dst[part, c, 0:HALF_ROWS] = top[s, l, part, :, lanes]
                dst[part, c, HALF_ROWS:low] = buf[s * local + l, part, :, lanes]
                dst[part, c, low:low + HALF_ROWS] = bot[s, l, part, :, lanes]

    def window(fields):
        count = len(fields)
        for f, field in enumerate(fields):
            pbuf[f] = field
        for f in range(count):
            sbuf[f, :, 0:span - 2] = (pbuf[f, :, 0:span - 2] + pbuf[f, :, 1:span - 1]) + pbuf[f, :, 2:span]
        for f in range(count):
            total = (sbuf[f, :, 0:height] + sbuf[f, :, 3:height + 3]) + sbuf[f, :, 6:height + 6]
            high = total.astype(jnp.bfloat16)
            low = (total - high.astype(jnp.float32)).astype(jnp.bfloat16)
            for c in range(tiles):
                lhs[f * height:(f + 1) * height, c * LANES:(c + 1) * LANES] = high[c]
                lhs[(count + f) * height:(count + f + 1) * height, c * LANES:(c + 1) * LANES] = low[c]
        sums = jnp.dot(lhs[0:2 * count * height], band[...], preferred_element_type=jnp.float32)
        return [sums[f * height:(f + 1) * height] + sums[(count + f) * height:(count + f + 1) * height]
                for f in range(count)]

    def local_power():
        fields = []
        for i in range(local):
            real, imag = mine[i, 0], mine[i, 1]
            fields.append(real * real + imag * imag)
        for i, power in enumerate(window(fields)):
            pw[i] = power

    def compute(s, l, oth):
        oth_real, oth_imag = oth[0], oth[1]
        fields = [oth_real * oth_real + oth_imag * oth_imag]
        for i in range(local):
            real, imag = mine[i, 0], mine[i, 1]
            fields.append(real * oth_real + imag * oth_imag)
            fields.append(imag * oth_real - real * oth_imag)
        sums = window(fields)
        date = s * local + l
        for i in range(local):
            factor = lax.rsqrt(pw[i] * sums[0] + epsilon)
            coh[i, date, 0] = sums[1 + 2 * i] * factor
            coh[i, date, 1] = sums[2 + 2 * i] * factor

    def own_dates():
        for l in range(local):
            wait_rims(me, l)
            assemble(mine.at[l], me, l)
        local_power()
        for l in range(local):
            compute(me, l, mine.at[l])

    def finish(s, l):
        wait_rims(s, l)
        assemble(other, s, l)
        compute(s, l, other)

    schedule, partners = chain_of_four() if n == 4 else ({}, {})
    held = {spot: [] for spot in schedule}
    pieces = {spot: [0, 0] for spot in schedule}

    def at(spot):
        return jnp.logical_and(me == spot[0], lax.rem(row, 2) == spot[1])

    def take(spot, s, k, l):
        if s != spot[0] and (s, k, l) not in held[spot]:
            held[spot].append((s, k, l))
            arrived(s, k, l)
            if k == EDGE:
                send_rims(s, l)

    def perform(spot, ops):
        here = spot[0]
        for op, *rest in ops:
            if op == "send":
                s, k, d = rest
                for l in range(local):
                    take(spot, s, k, l)
                    source = x_ref if s == here and d < here else buf.at[pl.ds(s * local, local)]
                    pieces[spot][d > here] += 1
                    send(source, s, k, l, d, int(d > here))
            elif op == "take":
                for l in range(local):
                    take(spot, rest[0], rest[1], l)
            elif op == "load":
                load.wait()
                for l in range(local):
                    pl.when(has_up)(lambda: rim_up(here, l).start())
            elif op == "down":
                @pl.when(has_down)
                def _():
                    pl.semaphore_wait(ready.at[1], 1)
                    for l in range(local):
                        rim_down(here, l).start()
            elif op == "right" and here < n - 1:
                pl.semaphore_wait(ready.at[0], 1)

    def everywhere(step):
        for spot in schedule:
            pl.when(at(spot))(functools.partial(step, spot))

    def short_chain():
        everywhere(lambda spot: perform(spot, schedule[spot][0]))
        prepare()
        everywhere(lambda spot: perform(spot, schedule[spot][1]))
        own_dates()
        for t in range(n - 1):
            everywhere(lambda spot: perform(spot, schedule[spot][2 + t]))
            s = functools.reduce(jnp.add, [jnp.where(me == d, partners[d][t], 0) for d in partners])
            for l in range(local):
                def rest(spot):
                    for k in (EDGE, MID):
                        for m in range(local) if k == EDGE else (l,):
                            take(spot, partners[spot[0]][t], k, m)

                everywhere(rest)
                finish(s, l)

        def drain(spot):
            for side in range(2):
                if pieces[spot][side]:
                    all_sent(side, pieces[spot][side] // 2)

        everywhere(drain)

    def long_chain():
        mine_now = buf.at[pl.ds(me * local, local)]
        chunks = [(k, l) for k in (EDGE, MID) for l in range(local)]

        @pl.when(has_left)
        def _():
            for k, l in chunks:
                send(x_ref, me, k, l, me - 1, me)

        load.wait()
        for l in range(local):
            pl.when(has_up)(lambda: rim_up(me, l).start())

        @pl.when(has_right)
        def _():
            pl.semaphore_wait(ready.at[0], 1)
            for k, l in chunks:
                send(mine_now, me, k, l, me + 1, n)

        @pl.when(has_down)
        def _():
            pl.semaphore_wait(ready.at[1], 1)
            for l in range(local):
                rim_down(me, l).start()

        prepare()

        def step(t, carry):
            s_left, s_right = me - 1 - t, me + 1 + t
            for k, l in chunks:
                for s, there, onward, to in ((s_right, s_right < n, has_left, me - 1), (s_left, s_left >= 0, has_right, me + 1)):
                    @pl.when(there)
                    def _():
                        arrived(s, k, l)
                        pl.when(onward)(lambda: send(buf.at[pl.ds(s * local, local)], s, k, l, to, s))
                        if k == EDGE:
                            send_rims(s, l)
            return carry

        lax.fori_loop(0, n - 1, step, 0)
        own_dates()

        def late(s, carry):
            @pl.when(s != me)
            def _():
                for l in range(local):
                    finish(s, l)
            return carry

        lax.fori_loop(0, n, late, 0)
        pl.when(has_left)(lambda: all_sent(me, local))
        pl.when(has_right)(lambda: all_sent(n, local))

        def drain(s, carry):
            passed = jnp.logical_or(jnp.logical_and(s > me, has_left), jnp.logical_and(s < me, has_right))
            pl.when(passed)(lambda: all_sent(s, local))
            return carry

        lax.fori_loop(0, n, drain, 0)

    if schedule:
        short_chain()
    else:
        long_chain()
    pl.when(has_down)(lambda: remote(top, top, rim_sent.at[0], rim_sent.at[0], "row", row).wait_send())
    pl.when(has_up)(lambda: remote(bot, bot, rim_sent.at[1], rim_sent.at[1], "row", row).wait_send())


def order_kernel(plan_ref, coh, out, sem):
    dates = out.shape[1]
    plan = plan_ref[...].reshape(1, dates)
    place = lax.broadcasted_iota(jnp.int32, (1, dates), 1)

    def copy(k):
        return pltpu.make_async_copy(coh.at[:, jnp.sum(jnp.where(place == k, plan, 0))], out.at[:, k], sem)

    def start(k, carry):
        copy(k).start()
        return carry

    if dates <= 8:
        for k in range(dates):
            start(k, 0)
    else:
        lax.fori_loop(0, dates, start, 0)
    pltpu.make_async_copy(coh, out, sem).wait()


def body(n, rows_n, stack_data, plan):
    local, _, height, width = stack_data.shape
    dates = local * n
    tiles = width // LANES
    fields = 2 * local + 1
    span = height + 2 * HALF_ROWS
    kind = jax.ShapeDtypeStruct((local, dates, 2, height, width), jnp.float32)
    dma = pltpu.SemaphoreType.DMA
    result_bytes = local * dates * 2 * height * width * 4
    stack_data = pltpu.with_memory_space_constraint(stack_data, pltpu.HBM)
    coh = pl.pallas_call(
        functools.partial(gather_kernel, n, rows_n),
        out_shape=kind,
        in_specs=[pl.BlockSpec(memory_space=pltpu.HBM)],
        out_specs=pl.BlockSpec(memory_space=pltpu.VMEM),
        scratch_shapes=[
            pltpu.VMEM((n * local, 2, height, width), jnp.float32),
            pltpu.VMEM((n, local, 2, HALF_ROWS, width), jnp.float32),
            pltpu.VMEM((n, local, 2, HALF_ROWS, width), jnp.float32),
            pltpu.VMEM((local, 2, tiles, span, LANES), jnp.float32),
            pltpu.VMEM((2, tiles, span, LANES), jnp.float32),
            pltpu.VMEM((width, width), jnp.bfloat16),
            pltpu.VMEM((fields, tiles, span, LANES), jnp.float32),
            pltpu.VMEM((fields, tiles, span, LANES), jnp.float32),
            pltpu.VMEM((2 * fields * height, width), jnp.bfloat16),
            pltpu.VMEM((local, height, width), jnp.float32),
            dma, pltpu.SemaphoreType.REGULAR((2,)),
            dma((n, 2, local)), dma((2,) if n == 4 else (n + 1,)), dma((2, n, local)), dma((2,)),
        ],
        compiler_params=pltpu.CompilerParams(
            collective_id=0, has_side_effects=True,
            vmem_limit_bytes=4 * result_bytes + (8 << 20)),
    )(stack_data)
    return pl.pallas_call(
        order_kernel,
        out_shape=kind,
        in_specs=[pl.BlockSpec(memory_space=pltpu.VMEM), pl.BlockSpec(memory_space=pltpu.VMEM)],
        out_specs=pl.BlockSpec(memory_space=pl.ANY),
        scratch_shapes=[dma],
        compiler_params=pltpu.CompilerParams(vmem_limit_bytes=2 * result_bytes + (2 << 20)),
    )(plan, coh)


def solution(mesh):
    placed = (P(("grp", "date"), None, "row", None), P())
    return jax.shard_map(
        functools.partial(body, mesh.shape["date"], mesh.shape["row"]),
        mesh=mesh,
        in_specs=placed,
        out_specs=P(("grp", "date"), None, None, "row", None),
        check_vma=False,
    )
```

```python
import functools

import jax
import jax.numpy as jnp
from jax import lax
from jax.experimental import pallas as pl
from jax.experimental.pallas import tpu as pltpu
from jax.sharding import PartitionSpec as P

HALF_ROWS = 4
HALF_COLS = 16
LANES = 128

epsilon = 1e-06

EDGE, MID = 0, 1


def chain_of_four():
    def send(s, k, d):
        return ("send", s, k, d)

    def take(s, k):
        return ("take", s, k)

    def right(d):
        return [("load",), ("down",), ("right",), send(d, EDGE, d + 1), send(d, MID, d + 1)]

    places = {}
    begin = right(0)
    places[0, 0] = [begin, [], [take(1, EDGE), take(2, EDGE)], [take(3, EDGE)], []]
    places[0, 1] = [begin, [], [take(1, EDGE)], [take(2, EDGE), take(3, EDGE)], []]
    begin = [send(1, EDGE, 0), send(1, MID, 0)] + right(1)
    places[1, 0] = [begin, [send(0, EDGE, 2), send(0, MID, 2)], [], [take(2, EDGE), take(3, EDGE)], []]
    places[1, 1] = [begin, [send(2, EDGE, 0), send(0, EDGE, 2), send(2, MID, 0), send(3, EDGE, 0), send(0, MID, 2),
                            send(3, MID, 0)], [], [], []]
    places[2, 0] = [[send(2, EDGE, 0), send(2, EDGE, 1), send(2, MID, 0)] + right(2),
                    [send(1, EDGE, 3), send(0, EDGE, 3), send(1, MID, 3), send(2, MID, 1), send(0, MID, 3),
                     take(3, EDGE)], [], [], []]
    places[2, 1] = [[send(2, EDGE, 1), send(2, MID, 1)] + right(2),
                    [send(3, EDGE, 1), send(1, EDGE, 3), send(3, MID, 1), send(0, EDGE, 3), send(1, MID, 3),
                     send(0, MID, 3)], [], [], []]
    places[3, 0] = [[send(3, EDGE, 0), send(3, EDGE, 2), send(3, MID, 0), send(3, MID, 2), send(3, EDGE, 1),
                     ("load",), ("down",)], [], [take(2, EDGE), take(1, EDGE), send(3, MID, 1)], [take(0, EDGE)], []]
    places[3, 1] = [[send(3, EDGE, 2), send(3, MID, 2), ("load",), ("down",)], [], [take(2, EDGE), take(1, EDGE)],
                    [take(0, EDGE)], []]
    return places, {0: (1, 2, 3), 1: (0, 2, 3), 2: (1, 0, 3), 3: (2, 1, 0)}


def pick(me, values):
    return functools.reduce(jnp.add, [jnp.where(me == d, value, 0) for d, value in values.items()])


def window(fields, band, pbuf, sbuf, lhs):
    count = len(fields)
    _, tiles, span, _ = pbuf.shape
    height = span - 2 * HALF_ROWS
    for f, field in enumerate(fields):
        pbuf[f] = field
    for f in range(count):
        sbuf[f, :, 0:span - 2] = (pbuf[f, :, 0:span - 2] + pbuf[f, :, 1:span - 1]) + pbuf[f, :, 2:span]
    for f in range(count):
        total = (sbuf[f, :, 0:height] + sbuf[f, :, 3:height + 3]) + sbuf[f, :, 6:height + 6]
        high = total.astype(jnp.bfloat16)
        low = (total - high.astype(jnp.float32)).astype(jnp.bfloat16)
        for c in range(tiles):
            lhs[f * height:(f + 1) * height, c * LANES:(c + 1) * LANES] = high[c]
            lhs[(count + f) * height:(count + f + 1) * height, c * LANES:(c + 1) * LANES] = low[c]
    sums = jnp.dot(lhs[0:2 * count * height], band[...], preferred_element_type=jnp.float32)
    return [sums[f * height:(f + 1) * height] + sums[(count + f) * height:(count + f + 1) * height]
            for f in range(count)]


def partner_results(mine, other, pw, dates, put, band, *work):
    local = mine.shape[0]
    fields = []
    for l in dates:
        real, imag = other[l, 0], other[l, 1]
        fields.append(real * real + imag * imag)
        for i in range(local):
            own_real, own_imag = mine[i, 0], mine[i, 1]
            fields.append(own_real * real + own_imag * imag)
            fields.append(own_imag * real - own_real * imag)
    sums = iter(window(fields, band, *work))
    for l in dates:
        power = next(sums)
        for i in range(local):
            factor = lax.rsqrt(pw[i] * power + epsilon)
            put(i, l, next(sums) * factor, next(sums) * factor)


def gather_kernel(n, rows_n, x_ref, coh, mine, other, pw, band, buf, top, bot, pbuf, sbuf, lhs,
                  load_sem, ready, recv, sent, rim_recv, rim_sent):
    local, _, height, width = x_ref.shape
    tiles = width // LANES
    me = lax.axis_index("date")
    row = lax.axis_index("row")
    has_left, has_right = me > 0, me < n - 1
    at_end = jnp.logical_not(jnp.logical_and(has_left, has_right))
    has_up, has_down = row > 0, row < rows_n - 1

    def count(*flags):
        return functools.reduce(jnp.add, [jnp.where(flag, 1, 0) for flag in flags])

    def tell(sem, axis, index):
        pl.semaphore_signal(sem, inc=1, device_id={axis: index}, device_id_type=pl.DeviceIdType.MESH)

    barrier = pltpu.get_barrier_semaphore()
    pl.when(has_down)(lambda: tell(barrier, "row", row + 1))
    load = pltpu.make_async_copy(x_ref, buf.at[pl.ds(me * local, local)], load_sem)
    load.start()
    pl.when(jnp.logical_or(has_left, has_up))(lambda: pl.semaphore_wait(barrier, count(has_left, has_up)))
    pl.when(has_right)(lambda: tell(barrier, "date", me + 1))
    pl.when(has_left)(lambda: tell(ready.at[0], "date", me - 1))
    pl.when(has_up)(lambda: tell(ready.at[1], "row", row - 1))

    def remote(src, dst, send_sem, recv_sem, axis, index):
        return pltpu.make_async_remote_copy(
            src_ref=src, dst_ref=dst, send_sem=send_sem, recv_sem=recv_sem,
            device_id={axis: index}, device_id_type=pl.DeviceIdType.MESH)

    upper, lower = slice(0, HALF_ROWS), slice(height - HALF_ROWS, height)
    middle = slice(HALF_ROWS, height - HALF_ROWS)
    both = slice(0, 2)
    pieces = {EDGE: (0,), MID: (1, 2)}
    areas = [[(both, upper), (both, lower)], [(slice(0, 1), middle)], [(slice(1, 2), middle)]]

    def send(source, s, p, l, d, sem):
        for part, rows in areas[p]:
            remote(source.at[l, part, rows], buf.at[s * local + l, part, rows], sent.at[sem], recv.at[s, p, l],
                   "date", d).start()

    def arrived(s, p, l):
        part, rows = areas[p][0] if p else (both, slice(0, 2 * HALF_ROWS))
        ref = buf.at[s * local + l, part, rows]
        remote(ref, ref, sent.at[0], recv.at[s, p, l], "date", me).wait_recv()

    def all_sent(sem, dates):
        ref = buf.at[pl.ds(0, dates)]
        remote(ref, ref, sent.at[sem], sent.at[sem], "date", me).wait_send()

    def dates_of(s):
        return buf.at[pl.ds(s * local, local)]

    def rim_down(s, l):
        return remote(buf.at[s * local + l, :, lower], top.at[s, l], rim_sent.at[0], rim_recv.at[0, s, l], "row", row + 1)

    def rim_up(s, l):
        return remote(buf.at[s * local + l, :, upper], bot.at[s, l], rim_sent.at[1], rim_recv.at[1, s, l], "row", row - 1)

    def send_rims(s, l):
        pl.when(has_down)(lambda: rim_down(s, l).start())
        pl.when(has_up)(lambda: rim_up(s, l).start())

    def own_rims_up():
        for l in range(local):
            pl.when(has_up)(lambda: rim_up(me, l).start())

    def own_rims_down():
        @pl.when(has_down)
        def _():
            pl.semaphore_wait(ready.at[1], 1)
            for l in range(local):
                rim_down(me, l).start()

    def prepare():
        @pl.when(row == 0)
        def _():
            top[...] = jnp.zeros_like(top)

        @pl.when(row == rows_n - 1)
        def _():
            bot[...] = jnp.zeros_like(bot)

        col_in = lax.broadcasted_iota(jnp.int32, (width, width), 0)
        col_out = lax.broadcasted_iota(jnp.int32, (width, width), 1)
        band[...] = jnp.where(jnp.abs(col_in - col_out) <= HALF_COLS, 1.0, 0.0).astype(jnp.bfloat16)

    def assemble(dst, s, l):
        pl.when(has_up)(lambda: rim_down(s, l).wait_recv())
        pl.when(has_down)(lambda: rim_up(s, l).wait_recv())
        low = height + HALF_ROWS
        for part in range(2):
            for c in range(tiles):
                lanes = slice(c * LANES, (c + 1) * LANES)
                dst[part, c, 0:HALF_ROWS] = top[s, l, part, :, lanes]
                dst[part, c, HALF_ROWS:low] = buf[s * local + l, part, :, lanes]
                dst[part, c, low:low + HALF_ROWS] = bot[s, l, part, :, lanes]

    def own_dates():
        for l in range(local):
            assemble(mine.at[l], me, l)
        pairs = [(i, j) for i in range(local) for j in range(i + 1, local)]
        fields = [mine[i, 0] * mine[i, 0] + mine[i, 1] * mine[i, 1] for i in range(local)]
        for i, j in pairs:
            fields.append(mine[i, 0] * mine[j, 0] + mine[i, 1] * mine[j, 1])
            fields.append(mine[i, 1] * mine[j, 0] - mine[i, 0] * mine[j, 1])
        sums = window(fields, band, pbuf, sbuf, lhs)

        def put(i, j, real, imag):
            factor = lax.rsqrt(sums[i] * sums[j] + epsilon)
            coh[i, me * local + j, 0] = real * factor
            coh[i, me * local + j, 1] = imag * factor

        for i in range(local):
            pw[i] = sums[i]
            put(i, i, sums[i], jnp.zeros_like(sums[i]))
        for f, (i, j) in enumerate(pairs):
            real, imag = sums[local + 2 * f], sums[local + 2 * f + 1]
            put(i, j, real, imag)
            put(j, i, real, -imag)

    def results(s, dates):
        for l in dates:
            assemble(other.at[l], s, l)

        def put(i, l, real, imag):
            coh[i, s * local + l, 0] = real
            coh[i, s * local + l, 1] = imag

        partner_results(mine, other, pw, dates, put, band, pbuf, sbuf, lhs)

    def short_chain():
        schedule, partners = chain_of_four()
        held = {place: set() for place in schedule}
        shares = {place: [0, 0] for place in schedule}

        def everywhere(step, *dates):
            for place in schedule:
                if place[0] in dates or not dates:
                    here = jnp.logical_and(me == place[0], lax.rem(row, 2) == place[1])
                    pl.when(here)(functools.partial(step, place))

        def take(place, s, k, l):
            for p in pieces[k]:
                if s != place[0] and (s, p, l) not in held[place]:
                    held[place].add((s, p, l))
                    arrived(s, p, l)
                    if k == EDGE:
                        send_rims(s, l)

        def perform(step, place):
            for op, *rest in schedule[place][step]:
                if op == "send":
                    s, k, d = rest
                    for l in range(local):
                        take(place, s, k, l)
                        for p in pieces[k]:
                            send(x_ref if s == place[0] and d < s else dates_of(s), s, p, l, d, int(d > place[0]))
                        shares[place][d > place[0]] += 1
                elif op == "take":
                    for l in range(local):
                        take(place, *rest, l)
                elif op == "load":
                    load.wait()
                    own_rims_up()
                elif op == "down":
                    own_rims_down()
                elif op == "right":
                    pl.semaphore_wait(ready.at[0], 1)

        everywhere(functools.partial(perform, 0))
        prepare()
        everywhere(functools.partial(perform, 1))
        own_dates()
        for t in range(n - 1):
            everywhere(functools.partial(perform, 2 + t))
            s = pick(me, {d: order[t] for d, order in partners.items()})

            def rest(ks, dates, place):
                for k in ks:
                    for l in dates:
                        take(place, partners[place[0]][t], k, l)

            @pl.when(at_end)
            def _():
                everywhere(functools.partial(rest, (EDGE,), range(local)), 0, n - 1)
                for l in range(local):
                    everywhere(functools.partial(rest, (MID,), (l,)), 0, n - 1)
                    results(s, (l,))

            @pl.when(jnp.logical_not(at_end))
            def _():
                everywhere(functools.partial(rest, (EDGE, MID), range(local)), *range(1, n - 1))
                results(s, tuple(range(local)))

        def drain(place):
            for side, share in enumerate(shares[place]):
                if share:
                    all_sent(side, share // 2)

        everywhere(drain)

    def long_chain():
        parts = [(p, l) for k in (EDGE, MID) for p in pieces[k] for l in range(local)]

        @pl.when(has_left)
        def _():
            for p, l in parts:
                send(x_ref, me, p, l, me - 1, me)

        load.wait()
        own_rims_up()

        @pl.when(has_right)
        def _():
            pl.semaphore_wait(ready.at[0], 1)
            for p, l in parts:
                send(dates_of(me), me, p, l, me + 1, n)

        own_rims_down()
        prepare()

        def relay(s, onward, to):
            for p, l in parts:
                arrived(s, p, l)
                pl.when(onward)(lambda: send(dates_of(s), s, p, l, to, s))
                if p == 0:
                    send_rims(s, l)

        def step(t, carry):
            s_left, s_right = me - 1 - t, me + 1 + t
            pl.when(s_right < n)(lambda: relay(s_right, has_left, me - 1))
            pl.when(s_left >= 0)(lambda: relay(s_left, has_right, me + 1))
            return carry

        lax.fori_loop(0, n - 1, step, 0)
        own_dates()

        def late(s, carry):
            @pl.when(s != me)
            def _():
                for l in range(local):
                    results(s, (l,))
            return carry

        lax.fori_loop(0, n, late, 0)
        pl.when(has_left)(lambda: all_sent(me, local))
        pl.when(has_right)(lambda: all_sent(n, local))

        def drain(s, carry):
            passed = jnp.logical_or(jnp.logical_and(s > me, has_left), jnp.logical_and(s < me, has_right))
            pl.when(passed)(lambda: all_sent(s, local))
            return carry

        lax.fori_loop(0, n, drain, 0)

    if n == 4:
        short_chain()
    else:
        long_chain()
    pl.when(has_down)(lambda: remote(top, top, rim_sent.at[0], rim_sent.at[0], "row", row).wait_send())
    pl.when(has_up)(lambda: remote(bot, bot, rim_sent.at[1], rim_sent.at[1], "row", row).wait_send())


def order_kernel(plan_ref, coh, out, sem):
    dates = out.shape[1]
    plan = plan_ref[...].reshape(1, dates)
    place = lax.broadcasted_iota(jnp.int32, (1, dates), 1)

    def start(k, carry):
        date = jnp.sum(jnp.where(place == k, plan, 0))
        pltpu.make_async_copy(coh.at[:, date], out.at[:, k], sem).start()
        return carry

    if dates <= 8:
        for k in range(dates):
            start(k, 0)
    else:
        lax.fori_loop(0, dates, start, 0)
    pltpu.make_async_copy(coh, out, sem).wait()


def body(n, rows_n, stack_data, plan):
    local, _, height, width = stack_data.shape
    dates = local * n
    tiles = width // LANES
    fields = (2 * local + 1) * local
    span = height + 2 * HALF_ROWS
    kind = jax.ShapeDtypeStruct((local, dates, 2, height, width), jnp.float32)
    dma = pltpu.SemaphoreType.DMA
    result_bytes = local * dates * 2 * height * width * 4
    stack_data = pltpu.with_memory_space_constraint(stack_data, pltpu.HBM)
    vmem = pl.BlockSpec(memory_space=pltpu.VMEM)
    coh = pl.pallas_call(
        functools.partial(gather_kernel, n, rows_n),
        out_shape=kind,
        in_specs=[pl.BlockSpec(memory_space=pltpu.HBM)],
        out_specs=vmem,
        scratch_shapes=[
            pltpu.VMEM((local, 2, tiles, span, LANES), jnp.float32),
            pltpu.VMEM((local, 2, tiles, span, LANES), jnp.float32),
            pltpu.VMEM((local, height, width), jnp.float32),
            pltpu.VMEM((width, width), jnp.bfloat16),
            pltpu.VMEM((n * local, 2, height, width), jnp.float32),
            pltpu.VMEM((n, local, 2, HALF_ROWS, width), jnp.float32),
            pltpu.VMEM((n, local, 2, HALF_ROWS, width), jnp.float32),
            pltpu.VMEM((fields, tiles, span, LANES), jnp.float32),
            pltpu.VMEM((fields, tiles, span, LANES), jnp.float32),
            pltpu.VMEM((2 * fields * height, width), jnp.bfloat16),
            dma, pltpu.SemaphoreType.REGULAR((2,)),
            dma((n, 3, local)), dma((2,) if n == 4 else (n + 1,)), dma((2, n, local)), dma((2,)),
        ],
        compiler_params=pltpu.CompilerParams(
            collective_id=0, has_side_effects=True,
            vmem_limit_bytes=4 * result_bytes + (8 << 20)),
    )(stack_data)
    return pl.pallas_call(
        order_kernel,
        out_shape=kind,
        in_specs=[vmem, vmem],
        out_specs=pl.BlockSpec(memory_space=pl.ANY),
        scratch_shapes=[dma],
        compiler_params=pltpu.CompilerParams(vmem_limit_bytes=2 * result_bytes + (2 << 20)),
    )(plan, coh)


def solution(mesh):
    placed = (P(("grp", "date"), None, "row", None), P())
    return jax.shard_map(
        functools.partial(body, mesh.shape["date"], mesh.shape["row"]),
        mesh=mesh,
        in_specs=placed,
        out_specs=P(("grp", "date"), None, None, "row", None),
        check_vma=False,
    )
```

```python
import functools

import jax
import jax.numpy as jnp
from jax import lax
from jax.experimental import pallas as pl
from jax.experimental.pallas import tpu as pltpu
from jax.sharding import PartitionSpec as P

HALF_ROWS = 4
HALF_COLS = 16
LANES = 128

epsilon = 1e-06

EDGE, MID = 0, 1


def chain_of_four():
    def send(s, k, d):
        return ("send", s, k, d)

    def take(s, k):
        return ("take", s, k)

    def right(d):
        return [("load",), ("down",), ("right",), send(d, EDGE, d + 1), send(d, MID, d + 1)]

    places = {}
    begin = right(0)
    places[0, 0] = [begin, [], [take(1, EDGE), take(2, EDGE)], [take(3, EDGE)], []]
    places[0, 1] = [begin, [], [take(1, EDGE)], [take(2, EDGE), take(3, EDGE)], []]
    begin = [send(1, EDGE, 0), send(1, MID, 0)] + right(1)
    places[1, 0] = [begin, [send(0, EDGE, 2), send(0, MID, 2)], [], [take(2, EDGE), take(3, EDGE)], []]
    places[1, 1] = [begin[:-1], [send(2, EDGE, 0), send(0, EDGE, 2), send(2, MID, 0), send(3, EDGE, 0), send(1, MID, 2),
                                 send(0, MID, 2), send(3, MID, 0)], [], [], []]
    places[2, 0] = [[send(2, EDGE, 0), send(2, EDGE, 1), send(2, MID, 0)] + right(2),
                    [send(1, EDGE, 3), send(0, EDGE, 3), send(1, MID, 3), send(2, MID, 1), send(0, MID, 3),
                     take(3, EDGE)], [], [], []]
    places[2, 1] = [[send(2, EDGE, 1), send(2, MID, 1)] + right(2)[:-1],
                    [send(3, EDGE, 1), send(1, EDGE, 3), send(3, MID, 1), send(0, EDGE, 3), send(2, MID, 3),
                     send(1, MID, 3), send(0, MID, 3)], [], [], []]
    places[3, 0] = [[send(3, EDGE, 0), send(3, EDGE, 2), send(3, MID, 0), send(3, MID, 2), send(3, EDGE, 1),
                     ("load",), ("down",)], [], [take(2, EDGE), take(1, EDGE), send(3, MID, 1)], [take(0, EDGE)], []]
    places[3, 1] = [[send(3, EDGE, 2), send(3, MID, 2), ("load",), ("down",)], [], [take(2, EDGE), take(1, EDGE)],
                    [take(0, EDGE)], []]
    return places, {0: (1, 2, 3), 1: (0, 2, 3), 2: (1, 0, 3), 3: (2, 1, 0)}


def pick(me, values):
    return functools.reduce(jnp.add, [jnp.where(me == d, value, 0) for d, value in values.items()])


def window(fields, band, pbuf, sbuf, lhs):
    count = len(fields)
    _, tiles, span, _ = pbuf.shape
    height = span - 2 * HALF_ROWS
    for f, field in enumerate(fields):
        pbuf[f] = field
    for f in range(count):
        sbuf[f, :, 0:span - 2] = (pbuf[f, :, 0:span - 2] + pbuf[f, :, 1:span - 1]) + pbuf[f, :, 2:span]
    for f in range(count):
        total = (sbuf[f, :, 0:height] + sbuf[f, :, 3:height + 3]) + sbuf[f, :, 6:height + 6]
        high = total.astype(jnp.bfloat16)
        low = (total - high.astype(jnp.float32)).astype(jnp.bfloat16)
        for c in range(tiles):
            lhs[f * height:(f + 1) * height, c * LANES:(c + 1) * LANES] = high[c]
            lhs[(count + f) * height:(count + f + 1) * height, c * LANES:(c + 1) * LANES] = low[c]
    sums = jnp.dot(lhs[0:2 * count * height], band[...], preferred_element_type=jnp.float32)
    return [sums[f * height:(f + 1) * height] + sums[(count + f) * height:(count + f + 1) * height]
            for f in range(count)]


def partner_results(mine, other, pw, dates, put, band, *work):
    local = mine.shape[0]
    fields = []
    for l in dates:
        real, imag = other[l, 0], other[l, 1]
        fields.append(real * real + imag * imag)
        for i in range(local):
            own_real, own_imag = mine[i, 0], mine[i, 1]
            fields.append(own_real * real + own_imag * imag)
            fields.append(own_imag * real - own_real * imag)
    sums = iter(window(fields, band, *work))
    for l in dates:
        power = next(sums)
        for i in range(local):
            factor = lax.rsqrt(pw[i] * power + epsilon)
            put(i, l, next(sums) * factor, next(sums) * factor)


def gather_kernel(n, rows_n, x_ref, coh, mine, other, pw, band, buf, top, bot, pbuf, sbuf, lhs,
                  load_sem, ready, recv, sent, rim_recv, rim_sent):
    local, _, height, width = x_ref.shape
    tiles = width // LANES
    me = lax.axis_index("date")
    row = lax.axis_index("row")
    has_left, has_right = me > 0, me < n - 1
    at_end = jnp.logical_not(jnp.logical_and(has_left, has_right))
    has_up, has_down = row > 0, row < rows_n - 1

    def count(*flags):
        return functools.reduce(jnp.add, [jnp.where(flag, 1, 0) for flag in flags])

    def tell(sem, axis, index):
        pl.semaphore_signal(sem, inc=1, device_id={axis: index}, device_id_type=pl.DeviceIdType.MESH)

    barrier = pltpu.get_barrier_semaphore()
    pl.when(has_down)(lambda: tell(barrier, "row", row + 1))
    load = pltpu.make_async_copy(x_ref, buf.at[pl.ds(me * local, local)], load_sem)
    load.start()
    pl.when(jnp.logical_or(has_left, has_up))(lambda: pl.semaphore_wait(barrier, count(has_left, has_up)))
    pl.when(has_right)(lambda: tell(barrier, "date", me + 1))
    pl.when(has_left)(lambda: tell(ready.at[0], "date", me - 1))
    pl.when(has_up)(lambda: tell(ready.at[1], "row", row - 1))

    def remote(src, dst, send_sem, recv_sem, axis, index):
        return pltpu.make_async_remote_copy(
            src_ref=src, dst_ref=dst, send_sem=send_sem, recv_sem=recv_sem,
            device_id={axis: index}, device_id_type=pl.DeviceIdType.MESH)

    upper, lower = slice(0, HALF_ROWS), slice(height - HALF_ROWS, height)
    middle = slice(HALF_ROWS, height - HALF_ROWS)
    both = slice(0, 2)
    pieces = {EDGE: (0,), MID: (1, 2)}
    areas = [[(both, upper), (both, lower)], [(slice(0, 1), middle)], [(slice(1, 2), middle)]]

    def landed(s, d, p, l):
        return recv.at[s - jnp.where(s > d, 1, 0), p, l]

    def send(source, s, p, l, d, sem):
        for part, rows in areas[p]:
            remote(source.at[l, part, rows], buf.at[s * local + l, part, rows], sent.at[sem], landed(s, d, p, l),
                   "date", d).start()

    def arrived(s, p, l):
        part, rows = areas[p][0] if p else (both, slice(0, 2 * HALF_ROWS))
        ref = buf.at[s * local + l, part, rows]
        remote(ref, ref, sent.at[0], landed(s, me, p, l), "date", me).wait_recv()

    def all_sent(sem, dates):
        ref = buf.at[pl.ds(0, dates)]
        remote(ref, ref, sent.at[sem], sent.at[sem], "date", me).wait_send()

    def dates_of(s):
        return buf.at[pl.ds(s * local, local)]

    def rim_down(s, l):
        return remote(buf.at[s * local + l, :, lower], top.at[s, l], rim_sent.at[0], rim_recv.at[0, s], "row", row + 1)

    def rim_up(s, l):
        return remote(buf.at[s * local + l, :, upper], bot.at[s, l], rim_sent.at[1], rim_recv.at[1, s], "row", row - 1)

    def send_rims(s, l):
        pl.when(has_down)(lambda: rim_down(s, l).start())
        pl.when(has_up)(lambda: rim_up(s, l).start())

    def own_rims_up():
        for l in range(local):
            pl.when(has_up)(lambda: rim_up(me, l).start())

    def own_rims_down():
        @pl.when(has_down)
        def _():
            pl.semaphore_wait(ready.at[1], 1)
            for l in range(local):
                rim_down(me, l).start()

    def prepare():
        @pl.when(row == 0)
        def _():
            top[...] = jnp.zeros_like(top)

        @pl.when(row == rows_n - 1)
        def _():
            bot[...] = jnp.zeros_like(bot)

        col_in = lax.broadcasted_iota(jnp.int32, (width, width), 0)
        col_out = lax.broadcasted_iota(jnp.int32, (width, width), 1)
        band[...] = jnp.where(jnp.abs(col_in - col_out) <= HALF_COLS, 1.0, 0.0).astype(jnp.bfloat16)

    def wait_rims(s):
        above, below = top.at[s], bot.at[s]
        pl.when(has_up)(lambda: remote(above, above, rim_sent.at[0], rim_recv.at[0, s], "row", row).wait_recv())
        pl.when(has_down)(lambda: remote(below, below, rim_sent.at[1], rim_recv.at[1, s], "row", row).wait_recv())

    def assemble(dst, s, l):
        low = height + HALF_ROWS
        for part in range(2):
            for c in range(tiles):
                lanes = slice(c * LANES, (c + 1) * LANES)
                dst[part, c, 0:HALF_ROWS] = top[s, l, part, :, lanes]
                dst[part, c, HALF_ROWS:low] = buf[s * local + l, part, :, lanes]
                dst[part, c, low:low + HALF_ROWS] = bot[s, l, part, :, lanes]

    def own_dates():
        wait_rims(me)
        for l in range(local):
            assemble(mine.at[l], me, l)
        pairs = [(i, j) for i in range(local) for j in range(i + 1, local)]
        fields = [mine[i, 0] * mine[i, 0] + mine[i, 1] * mine[i, 1] for i in range(local)]
        for i, j in pairs:
            fields.append(mine[i, 0] * mine[j, 0] + mine[i, 1] * mine[j, 1])
            fields.append(mine[i, 1] * mine[j, 0] - mine[i, 0] * mine[j, 1])
        sums = window(fields, band, pbuf, sbuf, lhs)

        def put(i, j, real, imag):
            factor = lax.rsqrt(sums[i] * sums[j] + epsilon)
            coh[i, me * local + j, 0] = real * factor
            coh[i, me * local + j, 1] = imag * factor

        for i in range(local):
            pw[i] = sums[i]
            put(i, i, sums[i], jnp.zeros_like(sums[i]))
        for f, (i, j) in enumerate(pairs):
            real, imag = sums[local + 2 * f], sums[local + 2 * f + 1]
            put(i, j, real, imag)
            put(j, i, real, -imag)

    def results(s, dates):
        if 0 in dates:
            wait_rims(s)
        for l in dates:
            assemble(other.at[l], s, l)

        def put(i, l, real, imag):
            coh[i, s * local + l, 0] = real
            coh[i, s * local + l, 1] = imag

        partner_results(mine, other, pw, dates, put, band, pbuf, sbuf, lhs)

    def short_chain():
        schedule, partners = chain_of_four()
        held = {place: set() for place in schedule}
        shares = {place: [0, 0] for place in schedule}

        def everywhere(step, *places):
            for place in schedule:
                if place in places or not places:
                    here = jnp.logical_and(me == place[0], lax.rem(row, 2) == place[1])
                    pl.when(here)(functools.partial(step, place))

        def take(place, s, k, l):
            for p in pieces[k]:
                if s != place[0] and (s, p, l) not in held[place]:
                    held[place].add((s, p, l))
                    arrived(s, p, l)
                    if k == EDGE:
                        send_rims(s, l)

        def perform(step, place):
            for op, *rest in schedule[place][step]:
                if op == "send":
                    s, k, d = rest
                    for l in range(local):
                        take(place, s, k, l)
                        for p in pieces[k]:
                            send(x_ref if s == place[0] and d < s else dates_of(s), s, p, l, d, int(d > place[0]))
                        shares[place][d > place[0]] += 1
                elif op == "take":
                    for l in range(local):
                        take(place, *rest, l)
                elif op == "load":
                    load.wait()
                    own_rims_up()
                elif op == "down":
                    own_rims_down()
                elif op == "right":
                    pl.semaphore_wait(ready.at[0], 1)

        everywhere(functools.partial(perform, 0))
        prepare()
        everywhere(functools.partial(perform, 1))
        own_dates()
        for t in range(n - 1):
            everywhere(functools.partial(perform, 2 + t))
            s = pick(me, {d: order[t] for d, order in partners.items()})

            def rest(ks, dates, place):
                for k in ks:
                    for l in dates:
                        take(place, partners[place[0]][t], k, l)

            singly = jnp.logical_and(at_end, lax.rem(row, 2) == 1)

            def pair():
                everywhere(functools.partial(rest, (EDGE, MID), range(local)), *pairing)
                results(s, tuple(range(local)))

            if t < n - 2:
                pairing = list(schedule)
                pair()
            else:
                alone = [place for place in schedule if place[0] in (0, n - 1) and place[1] == 1]
                pairing = [place for place in schedule if place not in alone]
                pl.when(jnp.logical_not(singly))(pair)

                @pl.when(singly)
                def _():
                    everywhere(functools.partial(rest, (EDGE,), range(local)), *alone)
                    for l in range(local):
                        everywhere(functools.partial(rest, (MID,), (l,)), *alone)
                        results(s, (l,))

        def drain(place):
            for side, share in enumerate(shares[place]):
                if share:
                    all_sent(side, share // 2)

        everywhere(drain)

    def long_chain():
        parts = [(p, l) for k in (EDGE, MID) for p in pieces[k] for l in range(local)]

        @pl.when(has_left)
        def _():
            for p, l in parts:
                send(x_ref, me, p, l, me - 1, me)

        load.wait()
        own_rims_up()

        @pl.when(has_right)
        def _():
            pl.semaphore_wait(ready.at[0], 1)
            for p, l in parts:
                send(dates_of(me), me, p, l, me + 1, n)

        own_rims_down()
        prepare()

        def relay(s, onward, to):
            for p, l in parts:
                arrived(s, p, l)
                pl.when(onward)(lambda: send(dates_of(s), s, p, l, to, s))
                if p == 0:
                    send_rims(s, l)

        def step(t, carry):
            s_left, s_right = me - 1 - t, me + 1 + t
            pl.when(s_right < n)(lambda: relay(s_right, has_left, me - 1))
            pl.when(s_left >= 0)(lambda: relay(s_left, has_right, me + 1))
            return carry

        lax.fori_loop(0, n - 1, step, 0)
        own_dates()

        def late(s, carry):
            @pl.when(s != me)
            def _():
                for l in range(local):
                    results(s, (l,))
            return carry

        lax.fori_loop(0, n, late, 0)
        pl.when(has_left)(lambda: all_sent(me, local))
        pl.when(has_right)(lambda: all_sent(n, local))

        def drain(s, carry):
            passed = jnp.logical_or(jnp.logical_and(s > me, has_left), jnp.logical_and(s < me, has_right))
            pl.when(passed)(lambda: all_sent(s, local))
            return carry

        lax.fori_loop(0, n, drain, 0)

    if n == 4:
        short_chain()
    else:
        long_chain()
    pl.when(has_down)(lambda: remote(top, top, rim_sent.at[0], rim_sent.at[0], "row", row).wait_send())
    pl.when(has_up)(lambda: remote(bot, bot, rim_sent.at[1], rim_sent.at[1], "row", row).wait_send())


def order_kernel(plan_ref, coh, out, sem):
    dates = out.shape[1]
    plan = plan_ref[...].reshape(1, dates)
    place = lax.broadcasted_iota(jnp.int32, (1, dates), 1)

    def start(k, carry):
        date = jnp.sum(jnp.where(place == k, plan, 0))
        pltpu.make_async_copy(coh.at[:, date], out.at[:, k], sem).start()
        return carry

    if dates <= 8:
        for k in range(dates):
            start(k, 0)
    else:
        lax.fori_loop(0, dates, start, 0)
    pltpu.make_async_copy(coh, out, sem).wait()


def body(n, rows_n, stack_data, plan):
    local, _, height, width = stack_data.shape
    dates = local * n
    tiles = width // LANES
    fields = (2 * local + 1) * local
    span = height + 2 * HALF_ROWS
    kind = jax.ShapeDtypeStruct((local, dates, 2, height, width), jnp.float32)
    dma = pltpu.SemaphoreType.DMA
    result_bytes = local * dates * 2 * height * width * 4
    stack_data = pltpu.with_memory_space_constraint(stack_data, pltpu.HBM)
    vmem = pl.BlockSpec(memory_space=pltpu.VMEM)
    coh = pl.pallas_call(
        functools.partial(gather_kernel, n, rows_n),
        out_shape=kind,
        in_specs=[pl.BlockSpec(memory_space=pltpu.HBM)],
        out_specs=vmem,
        scratch_shapes=[
            pltpu.VMEM((local, 2, tiles, span, LANES), jnp.float32),
            pltpu.VMEM((local, 2, tiles, span, LANES), jnp.float32),
            pltpu.VMEM((local, height, width), jnp.float32),
            pltpu.VMEM((width, width), jnp.bfloat16),
            pltpu.VMEM((n * local, 2, height, width), jnp.float32),
            pltpu.VMEM((n, local, 2, HALF_ROWS, width), jnp.float32),
            pltpu.VMEM((n, local, 2, HALF_ROWS, width), jnp.float32),
            pltpu.VMEM((fields, tiles, span, LANES), jnp.float32),
            pltpu.VMEM((fields, tiles, span, LANES), jnp.float32),
            pltpu.VMEM((2 * fields * height, width), jnp.bfloat16),
            dma, pltpu.SemaphoreType.REGULAR((2,)),
            dma((n - 1, 3, local)), dma((2,) if n == 4 else (n + 1,)), dma((2, n)), dma((2,)),
        ],
        compiler_params=pltpu.CompilerParams(
            collective_id=0, has_side_effects=True,
            vmem_limit_bytes=4 * result_bytes + (8 << 20)),
    )(stack_data)
    return pl.pallas_call(
        order_kernel,
        out_shape=kind,
        in_specs=[vmem, vmem],
        out_specs=pl.BlockSpec(memory_space=pl.ANY),
        scratch_shapes=[dma],
        compiler_params=pltpu.CompilerParams(vmem_limit_bytes=2 * result_bytes + (2 << 20)),
    )(plan, coh)


def solution(mesh):
    placed = (P(("grp", "date"), None, "row", None), P())
    return jax.shard_map(
        functools.partial(body, mesh.shape["date"], mesh.shape["row"]),
        mesh=mesh,
        in_specs=placed,
        out_specs=P(("grp", "date"), None, None, "row", None),
        check_vma=False,
    )
```

```python
import functools

import jax
import jax.numpy as jnp
from jax import lax
from jax.experimental import pallas as pl
from jax.experimental.pallas import tpu as pltpu
from jax.sharding import PartitionSpec as P

HALF_ROWS = 4
HALF_COLS = 16
LANES = 128

epsilon = 1e-06

EDGE, MID = 0, 1


def chain_of_four():
    def send(s, k, d):
        return ("send", s, k, d)

    def take(s, k):
        return ("take", s, k)

    def right(d):
        return [("load",), ("down",), ("right",), send(d, EDGE, d + 1), send(d, MID, d + 1)]

    places = {}
    begin = right(0)
    places[0, 0] = [begin, [], [take(1, EDGE), take(2, EDGE)], [take(3, EDGE)], []]
    places[0, 1] = [begin, [], [take(1, EDGE)], [take(2, EDGE), take(3, EDGE)], []]
    begin = [send(1, EDGE, 0), send(1, MID, 0)] + right(1)
    places[1, 0] = [begin, [send(0, EDGE, 2), send(0, MID, 2)], [], [take(2, EDGE), take(3, EDGE)], []]
    places[1, 1] = [begin[:-1], [send(2, EDGE, 0), send(0, EDGE, 2), send(2, MID, 0), send(3, EDGE, 0), send(1, MID, 2),
                                 send(0, MID, 2), send(3, MID, 0)], [], [], []]
    places[2, 0] = [[send(2, EDGE, 0), send(2, EDGE, 1), send(2, MID, 0)] + right(2),
                    [send(1, EDGE, 3), send(0, EDGE, 3), send(1, MID, 3), send(2, MID, 1), send(0, MID, 3),
                     take(3, EDGE)], [], [], []]
    places[2, 1] = [[send(2, EDGE, 1), send(2, MID, 1)] + right(2)[:-1],
                    [send(3, EDGE, 1), send(1, EDGE, 3), send(3, MID, 1), send(0, EDGE, 3), send(2, MID, 3),
                     send(1, MID, 3), send(0, MID, 3)], [], [], []]
    places[3, 0] = [[send(3, EDGE, 0), send(3, EDGE, 2), send(3, MID, 0), send(3, MID, 2), ("lower", 3, EDGE, 1),
                     ("load",), ("down",)], [], [take(2, EDGE), ("upper", 3, EDGE, 1), take(1, EDGE), send(3, MID, 1)],
                    [take(0, EDGE)], []]
    places[3, 1] = [[send(3, EDGE, 2), send(3, MID, 2), ("load",), ("down",)], [], [take(2, EDGE), take(1, EDGE)],
                    [take(0, EDGE)], []]
    return places, {0: (1, 2, 3), 1: (0, 2, 3), 2: (1, 0, 3), 3: (2, 1, 0)}


def pick(me, values):
    return functools.reduce(jnp.add, [jnp.where(me == d, value, 0) for d, value in values.items()])


def window(fields, band, pbuf, sbuf, lhs):
    count = len(fields)
    _, tiles, span, _ = pbuf.shape
    height = span - 2 * HALF_ROWS
    blocks, rows, half = tiles // 2, 2 * count * height, count * height
    for f, field in enumerate(fields):
        pbuf[f] = field
    for f in range(count):
        sbuf[f, :, 0:span - 2] = (pbuf[f, :, 0:span - 2] + pbuf[f, :, 1:span - 1]) + pbuf[f, :, 2:span]
    for f in range(count):
        total = (sbuf[f, :, 0:height] + sbuf[f, :, 3:height + 3]) + sbuf[f, :, 6:height + 6]
        high = total.astype(jnp.bfloat16)
        low = (total - high.astype(jnp.float32)).astype(jnp.bfloat16)
        for first, values in ((f * height, high), (half + f * height, low)):
            for c in range(tiles):
                block, side = c // 2, c % 2
                lhs[block * rows + first:block * rows + first + height, side * LANES:(side + 1) * LANES] = values[c]
                seam = (c - 1) // 2
                if 0 < c < tiles - 1:
                    start = (blocks + seam) * rows + first
                    lhs[start:start + height, (1 - side) * LANES:(2 - side) * LANES] = values[c]
    main = jnp.dot(lhs[0:blocks * rows], band[0:2 * LANES], preferred_element_type=jnp.float32)
    seams = jnp.dot(lhs[blocks * rows:(2 * blocks - 1) * rows], band[2 * LANES:4 * LANES], preferred_element_type=jnp.float32)
    columns = []
    for c in range(tiles):
        block, side = c // 2, c % 2
        lanes = slice(side * LANES, (side + 1) * LANES)
        value = main[block * rows:block * rows + half, lanes] + main[block * rows + half:(block + 1) * rows, lanes]
        if 0 < c < tiles - 1:
            start = (c - 1) // 2 * rows
            lanes = slice((1 - side) * LANES, (2 - side) * LANES)
            value = value + (seams[start:start + half, lanes] + seams[start + half:start + rows, lanes])
        columns.append(value)
    sums = jnp.concatenate(columns, axis=1)
    return [sums[f * height:(f + 1) * height] for f in range(count)]


def partner_results(mine, other, pw, dates, put, band, *work):
    local = mine.shape[0]
    fields = []
    for l in dates:
        real, imag = other[l, 0], other[l, 1]
        fields.append(real * real + imag * imag)
        for i in range(local):
            own_real, own_imag = mine[i, 0], mine[i, 1]
            fields.append(own_real * real + own_imag * imag)
            fields.append(own_imag * real - own_real * imag)
    sums = iter(window(fields, band, *work))
    for l in dates:
        power = next(sums)
        for i in range(local):
            factor = lax.rsqrt(pw[i] * power + epsilon)
            put(i, l, next(sums) * factor, next(sums) * factor)


def gather_kernel(n, rows_n, x_ref, coh, mine, other, pw, band, buf, top, bot, pbuf, sbuf, lhs,
                  load_sem, ready, recv, sent, rim_recv, rim_sent):
    local, _, height, width = x_ref.shape
    tiles = width // LANES
    me = lax.axis_index("date")
    row = lax.axis_index("row")
    has_left, has_right = me > 0, me < n - 1
    at_end = jnp.logical_not(jnp.logical_and(has_left, has_right))
    has_up, has_down = row > 0, row < rows_n - 1

    def count(*flags):
        return functools.reduce(jnp.add, [jnp.where(flag, 1, 0) for flag in flags])

    def tell(sem, axis, index):
        pl.semaphore_signal(sem, inc=1, device_id={axis: index}, device_id_type=pl.DeviceIdType.MESH)

    barrier = pltpu.get_barrier_semaphore()
    pl.when(has_down)(lambda: tell(barrier, "row", row + 1))
    load = pltpu.make_async_copy(x_ref, buf.at[pl.ds(me * local, local)], load_sem)
    load.start()
    pl.when(jnp.logical_or(has_left, has_up))(lambda: pl.semaphore_wait(barrier, count(has_left, has_up)))
    pl.when(has_right)(lambda: tell(barrier, "date", me + 1))
    pl.when(has_left)(lambda: tell(ready.at[0], "date", me - 1))
    pl.when(has_up)(lambda: tell(ready.at[1], "row", row - 1))

    def remote(src, dst, send_sem, recv_sem, axis, index):
        return pltpu.make_async_remote_copy(
            src_ref=src, dst_ref=dst, send_sem=send_sem, recv_sem=recv_sem,
            device_id={axis: index}, device_id_type=pl.DeviceIdType.MESH)

    upper, lower = slice(0, HALF_ROWS), slice(height - HALF_ROWS, height)
    middle = slice(HALF_ROWS, height - HALF_ROWS)
    both = slice(0, 2)
    pieces = {EDGE: (0,), MID: (1, 2)}
    areas = [[(both, upper), (both, lower)], [(slice(0, 1), middle)], [(slice(1, 2), middle)]]

    def landed(s, d, p, l):
        return recv.at[s - jnp.where(s > d, 1, 0), p, l]

    def send(source, s, p, l, d, sem):
        for part, rows in areas[p]:
            remote(source.at[l, part, rows], buf.at[s * local + l, part, rows], sent.at[sem], landed(s, d, p, l),
                   "date", d).start()

    def arrived(s, p, l):
        part, rows = areas[p][0] if p else (both, slice(0, 2 * HALF_ROWS))
        ref = buf.at[s * local + l, part, rows]
        remote(ref, ref, sent.at[0], landed(s, me, p, l), "date", me).wait_recv()

    def all_sent(sem, dates):
        ref = buf.at[pl.ds(0, dates)]
        remote(ref, ref, sent.at[sem], sent.at[sem], "date", me).wait_send()

    def dates_of(s):
        return buf.at[pl.ds(s * local, local)]

    def rim_down(s, l):
        return remote(buf.at[s * local + l, :, lower], top.at[s, l], rim_sent.at[0], rim_recv.at[0, s], "row", row + 1)

    def rim_up(s, l):
        return remote(buf.at[s * local + l, :, upper], bot.at[s, l], rim_sent.at[1], rim_recv.at[1, s], "row", row - 1)

    def send_rims(s, l):
        pl.when(has_down)(lambda: rim_down(s, l).start())
        pl.when(has_up)(lambda: rim_up(s, l).start())

    def own_rims_up():
        for l in range(local):
            pl.when(has_up)(lambda: rim_up(me, l).start())

    def own_rims_down():
        @pl.when(has_down)
        def _():
            pl.semaphore_wait(ready.at[1], 1)
            for l in range(local):
                rim_down(me, l).start()

    def prepare():
        @pl.when(row == 0)
        def _():
            top[...] = jnp.zeros_like(top)

        @pl.when(row == rows_n - 1)
        def _():
            bot[...] = jnp.zeros_like(bot)

        size = 2 * LANES
        col_in = lax.broadcasted_iota(jnp.int32, (size, size), 0)
        col_out = lax.broadcasted_iota(jnp.int32, (size, size), 1)
        near = jnp.abs(col_in - col_out) <= HALF_COLS
        across = jnp.logical_and(near, jnp.logical_xor(col_in < LANES, col_out < LANES))
        band[0:size] = jnp.where(near, 1.0, 0.0).astype(jnp.bfloat16)
        band[size:2 * size] = jnp.where(across, 1.0, 0.0).astype(jnp.bfloat16)

    def wait_rims(s):
        above, below = top.at[s], bot.at[s]
        pl.when(has_up)(lambda: remote(above, above, rim_sent.at[0], rim_recv.at[0, s], "row", row).wait_recv())
        pl.when(has_down)(lambda: remote(below, below, rim_sent.at[1], rim_recv.at[1, s], "row", row).wait_recv())

    def assemble(dst, s, l):
        low = height + HALF_ROWS
        for part in range(2):
            for c in range(tiles):
                lanes = slice(c * LANES, (c + 1) * LANES)
                dst[part, c, 0:HALF_ROWS] = top[s, l, part, :, lanes]
                dst[part, c, HALF_ROWS:low] = buf[s * local + l, part, :, lanes]
                dst[part, c, low:low + HALF_ROWS] = bot[s, l, part, :, lanes]

    def own_dates():
        wait_rims(me)
        for l in range(local):
            assemble(mine.at[l], me, l)
        pairs = [(i, j) for i in range(local) for j in range(i + 1, local)]
        fields = [mine[i, 0] * mine[i, 0] + mine[i, 1] * mine[i, 1] for i in range(local)]
        for i, j in pairs:
            fields.append(mine[i, 0] * mine[j, 0] + mine[i, 1] * mine[j, 1])
            fields.append(mine[i, 1] * mine[j, 0] - mine[i, 0] * mine[j, 1])
        sums = window(fields, band, pbuf, sbuf, lhs)

        def put(i, j, real, imag):
            factor = lax.rsqrt(sums[i] * sums[j] + epsilon)
            coh[i, me * local + j, 0] = real * factor
            coh[i, me * local + j, 1] = imag * factor

        for i in range(local):
            pw[i] = sums[i]
            put(i, i, sums[i], jnp.zeros_like(sums[i]))
        for f, (i, j) in enumerate(pairs):
            real, imag = sums[local + 2 * f], sums[local + 2 * f + 1]
            put(i, j, real, imag)
            put(j, i, real, -imag)

    def results(s, dates):
        if 0 in dates:
            wait_rims(s)
        for l in dates:
            assemble(other.at[l], s, l)

        def put(i, l, real, imag):
            coh[i, s * local + l, 0] = real
            coh[i, s * local + l, 1] = imag

        partner_results(mine, other, pw, dates, put, band, pbuf, sbuf, lhs)

    def short_chain():
        schedule, partners = chain_of_four()
        held = {place: set() for place in schedule}
        shares = {place: [0, 0] for place in schedule}

        def everywhere(step, *places):
            for place in schedule:
                if place in places or not places:
                    here = jnp.logical_and(me == place[0], lax.rem(row, 2) == place[1])
                    pl.when(here)(functools.partial(step, place))

        def take(place, s, k, l):
            for p in pieces[k]:
                if s != place[0] and (s, p, l) not in held[place]:
                    held[place].add((s, p, l))
                    arrived(s, p, l)
                    if k == EDGE:
                        send_rims(s, l)

        def perform(step, place):
            for op, *rest in schedule[place][step]:
                if op == "send":
                    s, k, d = rest
                    for l in range(local):
                        take(place, s, k, l)
                        for p in pieces[k]:
                            send(x_ref if s == place[0] and d < s else dates_of(s), s, p, l, d, int(d > place[0]))
                        shares[place][d > place[0]] += 1
                elif op in ("upper", "lower"):
                    s, k, d = rest

                    @pl.when((row < rows_n // 2) if op == "upper" else (row >= rows_n // 2))
                    def _():
                        for l in range(local):
                            for p in pieces[k]:
                                send(x_ref, s, p, l, d, 0)
                    shares[place][0] += local if op == "upper" else 0
                elif op == "take":
                    for l in range(local):
                        take(place, *rest, l)
                elif op == "load":
                    load.wait()
                    own_rims_up()
                elif op == "down":
                    own_rims_down()
                elif op == "right":
                    pl.semaphore_wait(ready.at[0], 1)

        everywhere(functools.partial(perform, 0))
        prepare()
        everywhere(functools.partial(perform, 1))
        own_dates()
        for t in range(n - 1):
            everywhere(functools.partial(perform, 2 + t))
            s = pick(me, {d: order[t] for d, order in partners.items()})

            def rest(ks, dates, place):
                for k in ks:
                    for l in dates:
                        take(place, partners[place[0]][t], k, l)

            singly = jnp.logical_and(at_end, lax.rem(row, 2) == 1)

            def pair():
                everywhere(functools.partial(rest, (EDGE, MID), range(local)), *pairing)
                results(s, tuple(range(local)))

            if t < n - 2:
                pairing = list(schedule)
                pair()
            else:
                alone = [place for place in schedule if place[0] in (0, n - 1) and place[1] == 1]
                pairing = [place for place in schedule if place not in alone]
                pl.when(jnp.logical_not(singly))(pair)

                @pl.when(singly)
                def _():
                    everywhere(functools.partial(rest, (EDGE,), range(local)), *alone)
                    for l in range(local):
                        everywhere(functools.partial(rest, (MID,), (l,)), *alone)
                        results(s, (l,))

        def drain(place):
            for side, share in enumerate(shares[place]):
                if share:
                    all_sent(side, share // 2)

        everywhere(drain)

    def long_chain():
        parts = [(p, l) for k in (EDGE, MID) for p in pieces[k] for l in range(local)]

        @pl.when(has_left)
        def _():
            for p, l in parts:
                send(x_ref, me, p, l, me - 1, me)

        load.wait()
        own_rims_up()

        @pl.when(has_right)
        def _():
            pl.semaphore_wait(ready.at[0], 1)
            for p, l in parts:
                send(dates_of(me), me, p, l, me + 1, n)

        own_rims_down()
        prepare()

        def relay(s, onward, to):
            for p, l in parts:
                arrived(s, p, l)
                pl.when(onward)(lambda: send(dates_of(s), s, p, l, to, s))
                if p == 0:
                    send_rims(s, l)

        def step(t, carry):
            s_left, s_right = me - 1 - t, me + 1 + t
            pl.when(s_right < n)(lambda: relay(s_right, has_left, me - 1))
            pl.when(s_left >= 0)(lambda: relay(s_left, has_right, me + 1))
            return carry

        lax.fori_loop(0, n - 1, step, 0)
        own_dates()

        def late(s, carry):
            @pl.when(s != me)
            def _():
                for l in range(local):
                    results(s, (l,))
            return carry

        lax.fori_loop(0, n, late, 0)
        pl.when(has_left)(lambda: all_sent(me, local))
        pl.when(has_right)(lambda: all_sent(n, local))

        def drain(s, carry):
            passed = jnp.logical_or(jnp.logical_and(s > me, has_left), jnp.logical_and(s < me, has_right))
            pl.when(passed)(lambda: all_sent(s, local))
            return carry

        lax.fori_loop(0, n, drain, 0)

    if n == 4:
        short_chain()
    else:
        long_chain()
    pl.when(has_down)(lambda: remote(top, top, rim_sent.at[0], rim_sent.at[0], "row", row).wait_send())
    pl.when(has_up)(lambda: remote(bot, bot, rim_sent.at[1], rim_sent.at[1], "row", row).wait_send())


def order_kernel(plan_ref, coh, out, sem):
    dates = out.shape[1]
    plan = plan_ref[...].reshape(1, dates)
    place = lax.broadcasted_iota(jnp.int32, (1, dates), 1)

    def start(k, carry):
        date = jnp.sum(jnp.where(place == k, plan, 0))
        pltpu.make_async_copy(coh.at[:, date], out.at[:, k], sem).start()
        return carry

    if dates <= 8:
        for k in range(dates):
            start(k, 0)
    else:
        lax.fori_loop(0, dates, start, 0)
    pltpu.make_async_copy(coh, out, sem).wait()


def body(n, rows_n, stack_data, plan):
    local, _, height, width = stack_data.shape
    dates = local * n
    tiles = width // LANES
    fields = (2 * local + 1) * local
    span = height + 2 * HALF_ROWS
    kind = jax.ShapeDtypeStruct((local, dates, 2, height, width), jnp.float32)
    dma = pltpu.SemaphoreType.DMA
    result_bytes = local * dates * 2 * height * width * 4
    stack_data = pltpu.with_memory_space_constraint(stack_data, pltpu.HBM)
    vmem = pl.BlockSpec(memory_space=pltpu.VMEM)
    coh = pl.pallas_call(
        functools.partial(gather_kernel, n, rows_n),
        out_shape=kind,
        in_specs=[pl.BlockSpec(memory_space=pltpu.HBM)],
        out_specs=vmem,
        scratch_shapes=[
            pltpu.VMEM((local, 2, tiles, span, LANES), jnp.float32),
            pltpu.VMEM((local, 2, tiles, span, LANES), jnp.float32),
            pltpu.VMEM((local, height, width), jnp.float32),
            pltpu.VMEM((4 * LANES, 2 * LANES), jnp.bfloat16),
            pltpu.VMEM((n * local, 2, height, width), jnp.float32),
            pltpu.VMEM((n, local, 2, HALF_ROWS, width), jnp.float32),
            pltpu.VMEM((n, local, 2, HALF_ROWS, width), jnp.float32),
            pltpu.VMEM((fields, tiles, span, LANES), jnp.float32),
            pltpu.VMEM((fields, tiles, span, LANES), jnp.float32),
            pltpu.VMEM((2 * fields * height * (tiles - 1), 2 * LANES), jnp.bfloat16),
            dma, pltpu.SemaphoreType.REGULAR((2,)),
            dma((n - 1, 3, local)), dma((2,) if n == 4 else (n + 1,)), dma((2, n)), dma((2,)),
        ],
        compiler_params=pltpu.CompilerParams(
            collective_id=0, has_side_effects=True,
            vmem_limit_bytes=4 * result_bytes + (8 << 20)),
    )(stack_data)
    return pl.pallas_call(
        order_kernel,
        out_shape=kind,
        in_specs=[vmem, vmem],
        out_specs=pl.BlockSpec(memory_space=pl.ANY),
        scratch_shapes=[dma],
        compiler_params=pltpu.CompilerParams(vmem_limit_bytes=2 * result_bytes + (2 << 20)),
    )(plan, coh)


def solution(mesh):
    placed = (P(("grp", "date"), None, "row", None), P())
    return jax.shard_map(
        functools.partial(body, mesh.shape["date"], mesh.shape["row"]),
        mesh=mesh,
        in_specs=placed,
        out_specs=P(("grp", "date"), None, None, "row", None),
        check_vma=False,
    )
```

```python
import functools

import jax
import jax.numpy as jnp
from jax import lax
from jax.experimental import pallas as pl
from jax.experimental.pallas import tpu as pltpu
from jax.sharding import PartitionSpec as P

HALF_ROWS = 4
HALF_COLS = 16
LANES = 128

epsilon = 1e-06

EDGE, MID = 0, 1


def chain_of_four():
    def send(s, k, d):
        return ("send", s, k, d)

    def take(s, k):
        return ("take", s, k)

    def right(d):
        return [("load",), ("down",), ("right",), send(d, EDGE, d + 1), send(d, MID, d + 1)]

    places = {}
    begin = right(0)
    places[0, 0] = [begin, [], [take(1, EDGE), take(2, EDGE)], [take(3, EDGE)], []]
    places[0, 1] = [begin, [], [take(1, EDGE)], [take(2, EDGE), take(3, EDGE)], []]
    begin = [send(1, EDGE, 0), send(1, MID, 0)] + right(1)
    places[1, 0] = [begin, [send(0, EDGE, 2), send(0, MID, 2)], [], [take(2, EDGE), take(3, EDGE)], []]
    places[1, 1] = [begin[:-1], [send(2, EDGE, 0), send(0, EDGE, 2), send(2, MID, 0), send(3, EDGE, 0), send(1, MID, 2),
                                 send(0, MID, 2), send(3, MID, 0)], [], [], []]
    places[2, 0] = [[send(2, EDGE, 0), send(2, EDGE, 1), send(2, MID, 0)] + right(2),
                    [send(1, EDGE, 3), send(0, EDGE, 3), send(1, MID, 3), send(2, MID, 1), send(0, MID, 3),
                     take(3, EDGE)], [], [], []]
    places[2, 1] = [[send(2, EDGE, 1), send(2, MID, 1)] + right(2)[:-1],
                    [send(3, EDGE, 1), send(1, EDGE, 3), send(3, MID, 1), send(0, EDGE, 3), send(2, MID, 3),
                     send(1, MID, 3), send(0, MID, 3)], [], [], []]
    places[3, 0] = [[send(3, EDGE, 0), send(3, EDGE, 2), send(3, MID, 0), send(3, MID, 2), ("lower", 3, EDGE, 1),
                     ("load",), ("down",)], [], [take(2, EDGE), ("upper", 3, EDGE, 1), take(1, EDGE), send(3, MID, 1)],
                    [take(0, EDGE)], []]
    places[3, 1] = [[send(3, EDGE, 2), send(3, MID, 2), ("load",), ("down",)], [], [take(2, EDGE), take(1, EDGE)],
                    [take(0, EDGE)], []]
    return places, {0: (1, 2, 3), 1: (0, 2, 3), 2: (1, 0, 3), 3: (2, 1, 0)}


def pick(me, values):
    return functools.reduce(jnp.add, [jnp.where(me == d, value, 0) for d, value in values.items()])


def window(fields, band, pbuf, sbuf, lhs):
    count = len(fields)
    _, tiles, span, _ = pbuf.shape
    height = span - 2 * HALF_ROWS
    blocks, rows, half = tiles // 2, 2 * count * height, count * height
    for f, field in enumerate(fields):
        pbuf[f] = field
    for f in range(count):
        sbuf[f, :, 0:span - 2] = (pbuf[f, :, 0:span - 2] + pbuf[f, :, 1:span - 1]) + pbuf[f, :, 2:span]
    for f in range(count):
        total = (sbuf[f, :, 0:height] + sbuf[f, :, 3:height + 3]) + sbuf[f, :, 6:height + 6]
        high = total.astype(jnp.bfloat16)
        low = (total - high.astype(jnp.float32)).astype(jnp.bfloat16)
        for first, values in ((f * height, high), (half + f * height, low)):
            for c in range(tiles):
                block, side = c // 2, c % 2
                lhs[block * rows + first:block * rows + first + height, side * LANES:(side + 1) * LANES] = values[c]
                seam = (c - 1) // 2
                if 0 < c < tiles - 1:
                    start = (blocks + seam) * rows + first
                    lhs[start:start + height, (1 - side) * LANES:(2 - side) * LANES] = values[c]
    main = jnp.dot(lhs[0:blocks * rows], band[0:2 * LANES], preferred_element_type=jnp.float32)
    seams = jnp.dot(lhs[blocks * rows:(2 * blocks - 1) * rows], band[2 * LANES:4 * LANES], preferred_element_type=jnp.float32)
    columns = []
    for c in range(tiles):
        block, side = c // 2, c % 2
        lanes = slice(side * LANES, (side + 1) * LANES)
        value = main[block * rows:block * rows + half, lanes] + main[block * rows + half:(block + 1) * rows, lanes]
        if 0 < c < tiles - 1:
            start = (c - 1) // 2 * rows
            lanes = slice((1 - side) * LANES, (2 - side) * LANES)
            value = value + (seams[start:start + half, lanes] + seams[start + half:start + rows, lanes])
        columns.append(value)
    sums = jnp.concatenate(columns, axis=1)
    return [sums[f * height:(f + 1) * height] for f in range(count)]


def partner_results(mine, other, pw, dates, put, band, *work):
    local = mine.shape[0]
    fields = []
    for l in dates:
        real, imag = other[l, 0], other[l, 1]
        fields.append(real * real + imag * imag)
        for i in range(local):
            own_real, own_imag = mine[i, 0], mine[i, 1]
            fields.append(own_real * real + own_imag * imag)
            fields.append(own_imag * real - own_real * imag)
    sums = iter(window(fields, band, *work))
    for l in dates:
        power = next(sums)
        for i in range(local):
            factor = lax.rsqrt(pw[i] * power + epsilon)
            put(i, l, next(sums) * factor, next(sums) * factor)


def gather_kernel(n, rows_n, x_ref, coh, mine, other, pw, band, buf, top, bot, pbuf, sbuf, lhs,
                  load_sem, ready, recv, sent, rim_recv, rim_sent):
    local, _, height, width = x_ref.shape
    tiles = width // LANES
    me = lax.axis_index("date")
    row = lax.axis_index("row")
    has_left, has_right = me > 0, me < n - 1
    at_end = jnp.logical_not(jnp.logical_and(has_left, has_right))
    has_up, has_down = row > 0, row < rows_n - 1

    def count(*flags):
        return functools.reduce(jnp.add, [jnp.where(flag, 1, 0) for flag in flags])

    def tell(sem, axis, index):
        pl.semaphore_signal(sem, inc=1, device_id={axis: index}, device_id_type=pl.DeviceIdType.MESH)

    barrier = pltpu.get_barrier_semaphore()
    pl.when(has_down)(lambda: tell(barrier, "row", row + 1))
    load = pltpu.make_async_copy(x_ref, buf.at[pl.ds(me * local, local)], load_sem)
    load.start()
    pl.when(jnp.logical_or(has_left, has_up))(lambda: pl.semaphore_wait(barrier, count(has_left, has_up)))
    pl.when(has_right)(lambda: tell(barrier, "date", me + 1))
    pl.when(has_left)(lambda: tell(ready.at[0], "date", me - 1))
    pl.when(has_up)(lambda: tell(ready.at[1], "row", row - 1))

    def remote(src, dst, send_sem, recv_sem, axis, index):
        return pltpu.make_async_remote_copy(
            src_ref=src, dst_ref=dst, send_sem=send_sem, recv_sem=recv_sem,
            device_id={axis: index}, device_id_type=pl.DeviceIdType.MESH)

    upper, lower = slice(0, HALF_ROWS), slice(height - HALF_ROWS, height)
    middle = slice(HALF_ROWS, height - HALF_ROWS)
    both = slice(0, 2)
    pieces = {EDGE: (0,), MID: (1,)}
    areas = [[(both, upper), (both, lower)], [(both, middle)]]

    def landed(s, d, p, l):
        return recv.at[s - jnp.where(s > d, 1, 0), p, l]

    def send(source, s, p, l, d, sem):
        for part, rows in areas[p]:
            remote(source.at[l, part, rows], buf.at[s * local + l, part, rows], sent.at[sem], landed(s, d, p, l),
                   "date", d).start()

    def arrived(s, p, l):
        part, rows = areas[p][0] if p else (both, slice(0, 2 * HALF_ROWS))
        ref = buf.at[s * local + l, part, rows]
        remote(ref, ref, sent.at[0], landed(s, me, p, l), "date", me).wait_recv()

    def all_sent(sem, dates):
        ref = buf.at[pl.ds(0, dates)]
        remote(ref, ref, sent.at[sem], sent.at[sem], "date", me).wait_send()

    def dates_of(s):
        return buf.at[pl.ds(s * local, local)]

    def rim_down(s, l):
        return remote(buf.at[s * local + l, :, lower], top.at[s, l], rim_sent.at[0], rim_recv.at[0, s], "row", row + 1)

    def rim_up(s, l):
        return remote(buf.at[s * local + l, :, upper], bot.at[s, l], rim_sent.at[1], rim_recv.at[1, s], "row", row - 1)

    def send_rims(s, l):
        pl.when(has_down)(lambda: rim_down(s, l).start())
        pl.when(has_up)(lambda: rim_up(s, l).start())

    def own_rims_up():
        for l in range(local):
            pl.when(has_up)(lambda: rim_up(me, l).start())

    def own_rims_down():
        @pl.when(has_down)
        def _():
            pl.semaphore_wait(ready.at[1], 1)
            for l in range(local):
                rim_down(me, l).start()

    def prepare():
        @pl.when(row == 0)
        def _():
            top[...] = jnp.zeros_like(top)

        @pl.when(row == rows_n - 1)
        def _():
            bot[...] = jnp.zeros_like(bot)

        size = 2 * LANES
        col_in = lax.broadcasted_iota(jnp.int32, (size, size), 0)
        col_out = lax.broadcasted_iota(jnp.int32, (size, size), 1)
        near = jnp.abs(col_in - col_out) <= HALF_COLS
        across = jnp.logical_and(near, jnp.logical_xor(col_in < LANES, col_out < LANES))
        band[0:size] = jnp.where(near, 1.0, 0.0).astype(jnp.bfloat16)
        band[size:2 * size] = jnp.where(across, 1.0, 0.0).astype(jnp.bfloat16)

    def wait_rims(s):
        above, below = top.at[s], bot.at[s]
        pl.when(has_up)(lambda: remote(above, above, rim_sent.at[0], rim_recv.at[0, s], "row", row).wait_recv())
        pl.when(has_down)(lambda: remote(below, below, rim_sent.at[1], rim_recv.at[1, s], "row", row).wait_recv())

    def assemble(dst, s, l):
        low = height + HALF_ROWS
        for part in range(2):
            for c in range(tiles):
                lanes = slice(c * LANES, (c + 1) * LANES)
                dst[part, c, 0:HALF_ROWS] = top[s, l, part, :, lanes]
                dst[part, c, HALF_ROWS:low] = buf[s * local + l, part, :, lanes]
                dst[part, c, low:low + HALF_ROWS] = bot[s, l, part, :, lanes]

    def own_dates():
        wait_rims(me)
        for l in range(local):
            assemble(mine.at[l], me, l)
        pairs = [(i, j) for i in range(local) for j in range(i + 1, local)]
        fields = [mine[i, 0] * mine[i, 0] + mine[i, 1] * mine[i, 1] for i in range(local)]
        for i, j in pairs:
            fields.append(mine[i, 0] * mine[j, 0] + mine[i, 1] * mine[j, 1])
            fields.append(mine[i, 1] * mine[j, 0] - mine[i, 0] * mine[j, 1])
        sums = window(fields, band, pbuf, sbuf, lhs)

        def put(i, j, real, imag):
            factor = lax.rsqrt(sums[i] * sums[j] + epsilon)
            coh[i, me * local + j, 0] = real * factor
            coh[i, me * local + j, 1] = imag * factor

        for i in range(local):
            pw[i] = sums[i]
            put(i, i, sums[i], jnp.zeros_like(sums[i]))
        for f, (i, j) in enumerate(pairs):
            real, imag = sums[local + 2 * f], sums[local + 2 * f + 1]
            put(i, j, real, imag)
            put(j, i, real, -imag)

    def results(s, dates):
        if 0 in dates:
            wait_rims(s)
        for l in dates:
            assemble(other.at[l], s, l)

        def put(i, l, real, imag):
            coh[i, s * local + l, 0] = real
            coh[i, s * local + l, 1] = imag

        partner_results(mine, other, pw, dates, put, band, pbuf, sbuf, lhs)

    def short_chain():
        schedule, partners = chain_of_four()
        held = {place: set() for place in schedule}
        shares = {place: [0, 0] for place in schedule}

        def everywhere(step, *places):
            for place in schedule:
                if place in places or not places:
                    here = jnp.logical_and(me == place[0], lax.rem(row, 2) == place[1])
                    pl.when(here)(functools.partial(step, place))

        def take(place, s, k, l):
            for p in pieces[k]:
                if s != place[0] and (s, p, l) not in held[place]:
                    held[place].add((s, p, l))
                    arrived(s, p, l)
                    if k == EDGE:
                        send_rims(s, l)

        def perform(step, place):
            for op, *rest in schedule[place][step]:
                if op == "send":
                    s, k, d = rest
                    for l in range(local):
                        take(place, s, k, l)
                        for p in pieces[k]:
                            send(x_ref if s == place[0] and d < s else dates_of(s), s, p, l, d, int(d > place[0]))
                        shares[place][d > place[0]] += 1
                elif op in ("upper", "lower"):
                    s, k, d = rest

                    @pl.when((row < rows_n // 2) if op == "upper" else (row >= rows_n // 2))
                    def _():
                        for l in range(local):
                            for p in pieces[k]:
                                send(x_ref, s, p, l, d, 0)
                    shares[place][0] += local if op == "upper" else 0
                elif op == "take":
                    for l in range(local):
                        take(place, *rest, l)
                elif op == "load":
                    load.wait()
                    own_rims_up()
                elif op == "down":
                    own_rims_down()
                elif op == "right":
                    pl.semaphore_wait(ready.at[0], 1)

        everywhere(functools.partial(perform, 0))
        prepare()
        everywhere(functools.partial(perform, 1))
        own_dates()
        for t in range(n - 1):
            everywhere(functools.partial(perform, 2 + t))
            s = pick(me, {d: order[t] for d, order in partners.items()})

            def rest(ks, dates, place):
                for k in ks:
                    for l in dates:
                        take(place, partners[place[0]][t], k, l)

            singly = jnp.logical_and(me == 0, lax.rem(row, 2) == 1)

            def pair():
                everywhere(functools.partial(rest, (EDGE, MID), range(local)), *pairing)
                results(s, tuple(range(local)))

            if t < n - 2:
                pairing = list(schedule)
                pair()
            else:
                alone = [place for place in schedule if place == (0, 1)]
                pairing = [place for place in schedule if place not in alone]
                pl.when(jnp.logical_not(singly))(pair)

                @pl.when(singly)
                def _():
                    everywhere(functools.partial(rest, (EDGE,), range(local)), *alone)
                    for l in range(local):
                        everywhere(functools.partial(rest, (MID,), (l,)), *alone)
                        results(s, (l,))

        def drain(place):
            for side, share in enumerate(shares[place]):
                if share:
                    all_sent(side, share // 2)

        everywhere(drain)

    def long_chain():
        parts = [(p, l) for k in (EDGE, MID) for p in pieces[k] for l in range(local)]

        @pl.when(has_left)
        def _():
            for p, l in parts:
                send(x_ref, me, p, l, me - 1, me)

        load.wait()
        own_rims_up()

        @pl.when(has_right)
        def _():
            pl.semaphore_wait(ready.at[0], 1)
            for p, l in parts:
                send(dates_of(me), me, p, l, me + 1, n)

        own_rims_down()
        prepare()

        def relay(s, onward, to):
            for p, l in parts:
                arrived(s, p, l)
                pl.when(onward)(lambda: send(dates_of(s), s, p, l, to, s))
                if p == 0:
                    send_rims(s, l)

        def step(t, carry):
            s_left, s_right = me - 1 - t, me + 1 + t
            pl.when(s_right < n)(lambda: relay(s_right, has_left, me - 1))
            pl.when(s_left >= 0)(lambda: relay(s_left, has_right, me + 1))
            return carry

        lax.fori_loop(0, n - 1, step, 0)
        own_dates()

        def late(s, carry):
            @pl.when(s != me)
            def _():
                for l in range(local):
                    results(s, (l,))
            return carry

        lax.fori_loop(0, n, late, 0)
        pl.when(has_left)(lambda: all_sent(me, local))
        pl.when(has_right)(lambda: all_sent(n, local))

        def drain(s, carry):
            passed = jnp.logical_or(jnp.logical_and(s > me, has_left), jnp.logical_and(s < me, has_right))
            pl.when(passed)(lambda: all_sent(s, local))
            return carry

        lax.fori_loop(0, n, drain, 0)

    if n == 4:
        short_chain()
    else:
        long_chain()
    pl.when(has_down)(lambda: remote(top, top, rim_sent.at[0], rim_sent.at[0], "row", row).wait_send())
    pl.when(has_up)(lambda: remote(bot, bot, rim_sent.at[1], rim_sent.at[1], "row", row).wait_send())


def order_kernel(plan_ref, coh, out, sem):
    dates = out.shape[1]
    plan = plan_ref[...].reshape(1, dates)
    place = lax.broadcasted_iota(jnp.int32, (1, dates), 1)

    def start(k, carry):
        date = jnp.sum(jnp.where(place == k, plan, 0))
        pltpu.make_async_copy(coh.at[:, date], out.at[:, k], sem).start()
        return carry

    if dates <= 8:
        for k in range(dates):
            start(k, 0)
    else:
        lax.fori_loop(0, dates, start, 0)
    pltpu.make_async_copy(coh, out, sem).wait()


def body(n, rows_n, stack_data, plan):
    local, _, height, width = stack_data.shape
    dates = local * n
    tiles = width // LANES
    fields = (2 * local + 1) * local
    span = height + 2 * HALF_ROWS
    kind = jax.ShapeDtypeStruct((local, dates, 2, height, width), jnp.float32)
    dma = pltpu.SemaphoreType.DMA
    result_bytes = local * dates * 2 * height * width * 4
    stack_data = pltpu.with_memory_space_constraint(stack_data, pltpu.HBM)
    vmem = pl.BlockSpec(memory_space=pltpu.VMEM)
    coh = pl.pallas_call(
        functools.partial(gather_kernel, n, rows_n),
        out_shape=kind,
        in_specs=[pl.BlockSpec(memory_space=pltpu.HBM)],
        out_specs=vmem,
        scratch_shapes=[
            pltpu.VMEM((local, 2, tiles, span, LANES), jnp.float32),
            pltpu.VMEM((local, 2, tiles, span, LANES), jnp.float32),
            pltpu.VMEM((local, height, width), jnp.float32),
            pltpu.VMEM((4 * LANES, 2 * LANES), jnp.bfloat16),
            pltpu.VMEM((n * local, 2, height, width), jnp.float32),
            pltpu.VMEM((n, local, 2, HALF_ROWS, width), jnp.float32),
            pltpu.VMEM((n, local, 2, HALF_ROWS, width), jnp.float32),
            pltpu.VMEM((fields, tiles, span, LANES), jnp.float32),
            pltpu.VMEM((fields, tiles, span, LANES), jnp.float32),
            pltpu.VMEM((2 * fields * height * (tiles - 1), 2 * LANES), jnp.bfloat16),
            dma, pltpu.SemaphoreType.REGULAR((2,)),
            dma((n - 1, 2, local)), dma((2,) if n == 4 else (n + 1,)), dma((2, n)), dma((2,)),
        ],
        compiler_params=pltpu.CompilerParams(
            collective_id=0, has_side_effects=True,
            vmem_limit_bytes=4 * result_bytes + (8 << 20)),
    )(stack_data)
    return pl.pallas_call(
        order_kernel,
        out_shape=kind,
        in_specs=[vmem, vmem],
        out_specs=pl.BlockSpec(memory_space=pl.ANY),
        scratch_shapes=[dma],
        compiler_params=pltpu.CompilerParams(vmem_limit_bytes=2 * result_bytes + (2 << 20)),
    )(plan, coh)


def solution(mesh):
    placed = (P(("grp", "date"), None, "row", None), P())
    return jax.shard_map(
        functools.partial(body, mesh.shape["date"], mesh.shape["row"]),
        mesh=mesh,
        in_specs=placed,
        out_specs=P(("grp", "date"), None, None, "row", None),
        check_vma=False,
    )
```

```python
import functools

import jax
import jax.numpy as jnp
from jax import lax
from jax.experimental import pallas as pl
from jax.experimental.pallas import tpu as pltpu
from jax.sharding import PartitionSpec as P

HALF_ROWS = 4
HALF_COLS = 16
LANES = 128

epsilon = 1e-06

EDGE, MID = 0, 1


def chain_of_four():
    def send(s, k, d):
        return ("send", s, k, d)

    def take(s, k):
        return ("take", s, k)

    def right(d):
        return [("load",), ("down",), ("right",), send(d, EDGE, d + 1), send(d, MID, d + 1)]

    places = {}
    begin = right(0)
    places[0, 0] = [begin, [], [take(1, EDGE), take(2, EDGE)], [take(3, EDGE)], []]
    places[0, 1] = [begin, [], [take(1, EDGE)], [take(2, EDGE), take(3, EDGE)], []]
    begin = [send(1, EDGE, 0), send(1, MID, 0)] + right(1)
    places[1, 0] = [begin, [send(0, EDGE, 2), send(0, MID, 2)], [], [take(2, EDGE), take(3, EDGE)], []]
    places[1, 1] = [begin[:-1] + [("upper", 1, MID, 2)],
                    [send(2, EDGE, 0), send(0, EDGE, 2), send(2, MID, 0), send(3, EDGE, 0), ("lower", 1, MID, 2),
                                 send(0, MID, 2), send(3, MID, 0)], [], [], []]
    places[2, 0] = [[send(2, EDGE, 0), send(2, EDGE, 1), send(2, MID, 0)] + right(2),
                    [send(1, EDGE, 3), send(0, EDGE, 3), send(1, MID, 3), send(2, MID, 1), send(0, MID, 3),
                     take(3, EDGE)], [], [], []]
    places[2, 1] = [[send(2, EDGE, 1), send(2, MID, 1)] + right(2)[:-1] + [("upper", 2, MID, 3)],
                    [send(3, EDGE, 1), send(1, EDGE, 3), send(3, MID, 1), send(0, EDGE, 3), ("lower", 2, MID, 3),
                     send(1, MID, 3), send(0, MID, 3)], [], [], []]
    places[3, 0] = [[send(3, EDGE, 0), send(3, EDGE, 2), send(3, MID, 0), send(3, MID, 2), ("lower", 3, EDGE, 1),
                     ("load",), ("down",)], [], [take(2, EDGE), ("upper", 3, EDGE, 1), take(1, EDGE), send(3, MID, 1)],
                    [take(0, EDGE)], []]
    places[3, 1] = [[send(3, EDGE, 2), send(3, MID, 2), ("load",), ("down",)], [], [take(2, EDGE), take(1, EDGE)],
                    [take(0, EDGE)], []]
    return places, {0: (1, 2, 3), 1: (0, 2, 3), 2: (1, 0, 3), 3: (2, 1, 0)}


def pick(me, values):
    return functools.reduce(jnp.add, [jnp.where(me == d, value, 0) for d, value in values.items()])


def window(fields, band, pbuf, sbuf, lhs):
    count = len(fields)
    _, tiles, span, _ = pbuf.shape
    height = span - 2 * HALF_ROWS
    blocks, rows, half = tiles // 2, 2 * count * height, count * height
    for f, field in enumerate(fields):
        pbuf[f] = field
    for f in range(count):
        sbuf[f, :, 0:span - 2] = (pbuf[f, :, 0:span - 2] + pbuf[f, :, 1:span - 1]) + pbuf[f, :, 2:span]
    for f in range(count):
        total = (sbuf[f, :, 0:height] + sbuf[f, :, 3:height + 3]) + sbuf[f, :, 6:height + 6]
        high = total.astype(jnp.bfloat16)
        low = (total - high.astype(jnp.float32)).astype(jnp.bfloat16)
        for first, values in ((f * height, high), (half + f * height, low)):
            for c in range(tiles):
                block, side = c // 2, c % 2
                lhs[block * rows + first:block * rows + first + height, side * LANES:(side + 1) * LANES] = values[c]
                seam = (c - 1) // 2
                if 0 < c < tiles - 1:
                    start = (blocks + seam) * rows + first
                    lhs[start:start + height, (1 - side) * LANES:(2 - side) * LANES] = values[c]
    main = jnp.dot(lhs[0:blocks * rows], band[0:2 * LANES], preferred_element_type=jnp.float32)
    seams = jnp.dot(lhs[blocks * rows:(2 * blocks - 1) * rows], band[2 * LANES:4 * LANES], preferred_element_type=jnp.float32)
    columns = []
    for c in range(tiles):
        block, side = c // 2, c % 2
        lanes = slice(side * LANES, (side + 1) * LANES)
        value = main[block * rows:block * rows + half, lanes] + main[block * rows + half:(block + 1) * rows, lanes]
        if 0 < c < tiles - 1:
            start = (c - 1) // 2 * rows
            lanes = slice((1 - side) * LANES, (2 - side) * LANES)
            value = value + (seams[start:start + half, lanes] + seams[start + half:start + rows, lanes])
        columns.append(value)
    sums = jnp.concatenate(columns, axis=1)
    return [sums[f * height:(f + 1) * height] for f in range(count)]


def partner_results(mine, other, pw, dates, put, band, *work):
    local = mine.shape[0]
    fields = []
    for l in dates:
        real, imag = other[l, 0], other[l, 1]
        fields.append(real * real + imag * imag)
        for i in range(local):
            own_real, own_imag = mine[i, 0], mine[i, 1]
            fields.append(own_real * real + own_imag * imag)
            fields.append(own_imag * real - own_real * imag)
    sums = iter(window(fields, band, *work))
    for l in dates:
        power = next(sums)
        for i in range(local):
            factor = lax.rsqrt(pw[i] * power + epsilon)
            put(i, l, next(sums) * factor, next(sums) * factor)


def gather_kernel(n, rows_n, x_ref, coh, mine, other, pw, band, buf, top, bot, pbuf, sbuf, lhs,
                  load_sem, ready, recv, sent, rim_recv, rim_sent):
    local, _, height, width = x_ref.shape
    tiles = width // LANES
    me = lax.axis_index("date")
    row = lax.axis_index("row")
    has_left, has_right = me > 0, me < n - 1
    at_end = jnp.logical_not(jnp.logical_and(has_left, has_right))
    has_up, has_down = row > 0, row < rows_n - 1

    def count(*flags):
        return functools.reduce(jnp.add, [jnp.where(flag, 1, 0) for flag in flags])

    def tell(sem, axis, index):
        pl.semaphore_signal(sem, inc=1, device_id={axis: index}, device_id_type=pl.DeviceIdType.MESH)

    barrier = pltpu.get_barrier_semaphore()
    pl.when(has_down)(lambda: tell(barrier, "row", row + 1))
    load = pltpu.make_async_copy(x_ref, buf.at[pl.ds(me * local, local)], load_sem)
    load.start()
    pl.when(jnp.logical_or(has_left, has_up))(lambda: pl.semaphore_wait(barrier, count(has_left, has_up)))
    pl.when(has_right)(lambda: tell(barrier, "date", me + 1))
    pl.when(has_left)(lambda: tell(ready.at[0], "date", me - 1))
    pl.when(has_up)(lambda: tell(ready.at[1], "row", row - 1))

    def remote(src, dst, send_sem, recv_sem, axis, index):
        return pltpu.make_async_remote_copy(
            src_ref=src, dst_ref=dst, send_sem=send_sem, recv_sem=recv_sem,
            device_id={axis: index}, device_id_type=pl.DeviceIdType.MESH)

    upper, lower = slice(0, HALF_ROWS), slice(height - HALF_ROWS, height)
    middle = slice(HALF_ROWS, height - HALF_ROWS)
    both = slice(0, 2)
    pieces = {EDGE: (0,), MID: (1,)}
    areas = [[(both, upper), (both, lower)], [(both, middle)]]

    def landed(s, d, p, l):
        return recv.at[s - jnp.where(s > d, 1, 0), p, l]

    def send(source, s, p, l, d, sem):
        for part, rows in areas[p]:
            remote(source.at[l, part, rows], buf.at[s * local + l, part, rows], sent.at[sem], landed(s, d, p, l),
                   "date", d).start()

    def arrived(s, p, l):
        part, rows = areas[p][0] if p else (both, slice(0, 2 * HALF_ROWS))
        ref = buf.at[s * local + l, part, rows]
        remote(ref, ref, sent.at[0], landed(s, me, p, l), "date", me).wait_recv()

    def all_sent(sem, dates):
        ref = buf.at[pl.ds(0, dates)]
        remote(ref, ref, sent.at[sem], sent.at[sem], "date", me).wait_send()

    def dates_of(s):
        return buf.at[pl.ds(s * local, local)]

    def rim_down(s, l):
        return remote(buf.at[s * local + l, :, lower], top.at[s, l], rim_sent.at[0], rim_recv.at[0, s], "row", row + 1)

    def rim_up(s, l):
        return remote(buf.at[s * local + l, :, upper], bot.at[s, l], rim_sent.at[1], rim_recv.at[1, s], "row", row - 1)

    def send_rims(s, l):
        pl.when(has_down)(lambda: rim_down(s, l).start())
        pl.when(has_up)(lambda: rim_up(s, l).start())

    def own_rims_up():
        for l in range(local):
            pl.when(has_up)(lambda: rim_up(me, l).start())

    def own_rims_down():
        @pl.when(has_down)
        def _():
            pl.semaphore_wait(ready.at[1], 1)
            for l in range(local):
                rim_down(me, l).start()

    def prepare():
        @pl.when(row == 0)
        def _():
            top[...] = jnp.zeros_like(top)

        @pl.when(row == rows_n - 1)
        def _():
            bot[...] = jnp.zeros_like(bot)

        size = 2 * LANES
        col_in = lax.broadcasted_iota(jnp.int32, (size, size), 0)
        col_out = lax.broadcasted_iota(jnp.int32, (size, size), 1)
        near = jnp.abs(col_in - col_out) <= HALF_COLS
        across = jnp.logical_and(near, jnp.logical_xor(col_in < LANES, col_out < LANES))
        band[0:size] = jnp.where(near, 1.0, 0.0).astype(jnp.bfloat16)
        band[size:2 * size] = jnp.where(across, 1.0, 0.0).astype(jnp.bfloat16)

    def wait_rims(s):
        above, below = top.at[s], bot.at[s]
        pl.when(has_up)(lambda: remote(above, above, rim_sent.at[0], rim_recv.at[0, s], "row", row).wait_recv())
        pl.when(has_down)(lambda: remote(below, below, rim_sent.at[1], rim_recv.at[1, s], "row", row).wait_recv())

    def assemble(dst, s, l):
        low = height + HALF_ROWS
        for part in range(2):
            for c in range(tiles):
                lanes = slice(c * LANES, (c + 1) * LANES)
                dst[part, c, 0:HALF_ROWS] = top[s, l, part, :, lanes]
                dst[part, c, HALF_ROWS:low] = buf[s * local + l, part, :, lanes]
                dst[part, c, low:low + HALF_ROWS] = bot[s, l, part, :, lanes]

    def own_dates():
        wait_rims(me)
        for l in range(local):
            assemble(mine.at[l], me, l)
        pairs = [(i, j) for i in range(local) for j in range(i + 1, local)]
        fields = [mine[i, 0] * mine[i, 0] + mine[i, 1] * mine[i, 1] for i in range(local)]
        for i, j in pairs:
            fields.append(mine[i, 0] * mine[j, 0] + mine[i, 1] * mine[j, 1])
            fields.append(mine[i, 1] * mine[j, 0] - mine[i, 0] * mine[j, 1])
        sums = window(fields, band, pbuf, sbuf, lhs)

        def put(i, j, real, imag):
            factor = lax.rsqrt(sums[i] * sums[j] + epsilon)
            coh[i, me * local + j, 0] = real * factor
            coh[i, me * local + j, 1] = imag * factor

        for i in range(local):
            pw[i] = sums[i]
            put(i, i, sums[i], jnp.zeros_like(sums[i]))
        for f, (i, j) in enumerate(pairs):
            real, imag = sums[local + 2 * f], sums[local + 2 * f + 1]
            put(i, j, real, imag)
            put(j, i, real, -imag)

    def results(s, dates):
        if 0 in dates:
            wait_rims(s)
        for l in dates:
            assemble(other.at[l], s, l)

        def put(i, l, real, imag):
            coh[i, s * local + l, 0] = real
            coh[i, s * local + l, 1] = imag

        partner_results(mine, other, pw, dates, put, band, pbuf, sbuf, lhs)

    def short_chain():
        schedule, partners = chain_of_four()
        held = {place: set() for place in schedule}
        shares = {place: [0, 0] for place in schedule}

        def everywhere(step, *places):
            for place in schedule:
                if place in places or not places:
                    here = jnp.logical_and(me == place[0], lax.rem(row, 2) == place[1])
                    pl.when(here)(functools.partial(step, place))

        def take(place, s, k, l):
            for p in pieces[k]:
                if s != place[0] and (s, p, l) not in held[place]:
                    held[place].add((s, p, l))
                    arrived(s, p, l)
                    if k == EDGE:
                        send_rims(s, l)

        def perform(step, place):
            for op, *rest in schedule[place][step]:
                if op == "send":
                    s, k, d = rest
                    for l in range(local):
                        take(place, s, k, l)
                        for p in pieces[k]:
                            send(x_ref if s == place[0] and d < s else dates_of(s), s, p, l, d, int(d > place[0]))
                        shares[place][d > place[0]] += 1
                elif op in ("upper", "lower"):
                    s, k, d = rest

                    @pl.when((row < rows_n // 2) if op == "upper" else (row >= rows_n // 2))
                    def _():
                        for l in range(local):
                            for p in pieces[k]:
                                send(x_ref if d < s else dates_of(s), s, p, l, d, int(d > s))
                    shares[place][d > s] += local if op == "upper" else 0
                elif op == "take":
                    for l in range(local):
                        take(place, *rest, l)
                elif op == "load":
                    load.wait()
                    own_rims_up()
                elif op == "down":
                    own_rims_down()
                elif op == "right":
                    pl.semaphore_wait(ready.at[0], 1)

        everywhere(functools.partial(perform, 0))
        prepare()
        everywhere(functools.partial(perform, 1))
        own_dates()
        for t in range(n - 1):
            everywhere(functools.partial(perform, 2 + t))
            s = pick(me, {d: order[t] for d, order in partners.items()})

            def rest(ks, dates, place):
                for k in ks:
                    for l in dates:
                        take(place, partners[place[0]][t], k, l)

            singly = jnp.logical_and(me == 0, lax.rem(row, 2) == 1)

            def pair():
                everywhere(functools.partial(rest, (EDGE, MID), range(local)), *pairing)
                results(s, tuple(range(local)))

            if t < n - 2:
                pairing = list(schedule)
                pair()
            else:
                alone = [place for place in schedule if place == (0, 1)]
                pairing = [place for place in schedule if place not in alone]
                pl.when(jnp.logical_not(singly))(pair)

                @pl.when(singly)
                def _():
                    everywhere(functools.partial(rest, (EDGE,), range(local)), *alone)
                    for l in range(local):
                        everywhere(functools.partial(rest, (MID,), (l,)), *alone)
                        results(s, (l,))

        def drain(place):
            for side, share in enumerate(shares[place]):
                if share:
                    all_sent(side, share // 2)

        everywhere(drain)

    def long_chain():
        parts = [(p, l) for k in (EDGE, MID) for p in pieces[k] for l in range(local)]

        @pl.when(has_left)
        def _():
            for p, l in parts:
                send(x_ref, me, p, l, me - 1, me)

        load.wait()
        own_rims_up()

        @pl.when(has_right)
        def _():
            pl.semaphore_wait(ready.at[0], 1)
            for p, l in parts:
                send(dates_of(me), me, p, l, me + 1, n)

        own_rims_down()
        prepare()

        def relay(s, onward, to):
            for p, l in parts:
                arrived(s, p, l)
                pl.when(onward)(lambda: send(dates_of(s), s, p, l, to, s))
                if p == 0:
                    send_rims(s, l)

        def step(t, carry):
            s_left, s_right = me - 1 - t, me + 1 + t
            pl.when(s_right < n)(lambda: relay(s_right, has_left, me - 1))
            pl.when(s_left >= 0)(lambda: relay(s_left, has_right, me + 1))
            return carry

        lax.fori_loop(0, n - 1, step, 0)
        own_dates()

        def late(s, carry):
            @pl.when(s != me)
            def _():
                for l in range(local):
                    results(s, (l,))
            return carry

        lax.fori_loop(0, n, late, 0)
        pl.when(has_left)(lambda: all_sent(me, local))
        pl.when(has_right)(lambda: all_sent(n, local))

        def drain(s, carry):
            passed = jnp.logical_or(jnp.logical_and(s > me, has_left), jnp.logical_and(s < me, has_right))
            pl.when(passed)(lambda: all_sent(s, local))
            return carry

        lax.fori_loop(0, n, drain, 0)

    if n == 4:
        short_chain()
    else:
        long_chain()
    pl.when(has_down)(lambda: remote(top, top, rim_sent.at[0], rim_sent.at[0], "row", row).wait_send())
    pl.when(has_up)(lambda: remote(bot, bot, rim_sent.at[1], rim_sent.at[1], "row", row).wait_send())


def order_kernel(plan_ref, coh, out, sem):
    dates = out.shape[1]
    plan = plan_ref[...].reshape(1, dates)
    place = lax.broadcasted_iota(jnp.int32, (1, dates), 1)

    def start(k, carry):
        date = jnp.sum(jnp.where(place == k, plan, 0))
        pltpu.make_async_copy(coh.at[:, date], out.at[:, k], sem).start()
        return carry

    if dates <= 8:
        for k in range(dates):
            start(k, 0)
    else:
        lax.fori_loop(0, dates, start, 0)
    pltpu.make_async_copy(coh, out, sem).wait()


def body(n, rows_n, stack_data, plan):
    local, _, height, width = stack_data.shape
    dates = local * n
    tiles = width // LANES
    fields = (2 * local + 1) * local
    span = height + 2 * HALF_ROWS
    kind = jax.ShapeDtypeStruct((local, dates, 2, height, width), jnp.float32)
    dma = pltpu.SemaphoreType.DMA
    result_bytes = local * dates * 2 * height * width * 4
    stack_data = pltpu.with_memory_space_constraint(stack_data, pltpu.HBM)
    vmem = pl.BlockSpec(memory_space=pltpu.VMEM)
    coh = pl.pallas_call(
        functools.partial(gather_kernel, n, rows_n),
        out_shape=kind,
        in_specs=[pl.BlockSpec(memory_space=pltpu.HBM)],
        out_specs=vmem,
        scratch_shapes=[
            pltpu.VMEM((local, 2, tiles, span, LANES), jnp.float32),
            pltpu.VMEM((local, 2, tiles, span, LANES), jnp.float32),
            pltpu.VMEM((local, height, width), jnp.float32),
            pltpu.VMEM((4 * LANES, 2 * LANES), jnp.bfloat16),
            pltpu.VMEM((n * local, 2, height, width), jnp.float32),
            pltpu.VMEM((n, local, 2, HALF_ROWS, width), jnp.float32),
            pltpu.VMEM((n, local, 2, HALF_ROWS, width), jnp.float32),
            pltpu.VMEM((fields, tiles, span, LANES), jnp.float32),
            pltpu.VMEM((fields, tiles, span, LANES), jnp.float32),
            pltpu.VMEM((2 * fields * height * (tiles - 1), 2 * LANES), jnp.bfloat16),
            dma, pltpu.SemaphoreType.REGULAR((2,)),
            dma((n - 1, 2, local)), dma((2,) if n == 4 else (n + 1,)), dma((2, n)), dma((2,)),
        ],
        compiler_params=pltpu.CompilerParams(
            collective_id=0, has_side_effects=True,
            vmem_limit_bytes=4 * result_bytes + (8 << 20)),
    )(stack_data)
    return pl.pallas_call(
        order_kernel,
        out_shape=kind,
        in_specs=[vmem, vmem],
        out_specs=pl.BlockSpec(memory_space=pl.ANY),
        scratch_shapes=[dma],
        compiler_params=pltpu.CompilerParams(vmem_limit_bytes=2 * result_bytes + (2 << 20)),
    )(plan, coh)


def solution(mesh):
    placed = (P(("grp", "date"), None, "row", None), P())
    return jax.shard_map(
        functools.partial(body, mesh.shape["date"], mesh.shape["row"]),
        mesh=mesh,
        in_specs=placed,
        out_specs=P(("grp", "date"), None, None, "row", None),
        check_vma=False,
    )
```
